512 devices in a mesh: blk: 16 (over z, x_lo), member: 32 (over y, x_hi, core).
Axes of the slice: x: 4 (x_hi: 2, x_lo: 2; x = x_hi * 2 + x_lo), y: 8, z: 8, core: 2. Of those that a mesh axis runs over, the one named last changes fastest.
Arguments:
- tokens: bfloat16 [32, 32, 4096], P('member', 'blk'), may hold values from -6 to 6
- cotangent: bfloat16 [32, 32, 4096], P('member', 'blk'), may hold values from -6 to 6
- routes: int32 [32, 32, 8], P('member'), may hold values from 0 to 63, all different within a row; in each aligned block of 32 rows (0 to 31, 32 to 63, ..., all dimensions but the last counted through in order) at most 6 rows name the same one
- gate_wts: float32 [32, 32, 8], P('member'), may hold values from 0.2 to 1
- w_gate: bfloat16 [16, 4096, 4096], P('blk', 'member'), may hold values from -0.09375 to 0.09375
- w_up: bfloat16 [16, 4096, 4096], P('blk', 'member'), may hold values from -0.09375 to 0.09375
- w_down: bfloat16 [16, 4096, 4096], P('blk', 'member'), may hold values from -0.1875 to 0.1875
Outputs:
- layer_out: bfloat16 [32, 32, 4096], P('member', 'blk')
- grad_in: bfloat16 [32, 32, 4096], P('member', 'blk')
The draws below stay inside these ranges and needn't reach their ends.
Inputs may be any that keep to these rules, and one draw needn't show every extreme that they name: `routes`: each token names 8 different experts. Within one token column (the 32 tokens of one index of the first dimension) no expert is named by more than 6 tokens, and in every draw some expert is named by exactly 6 tokens of some column.
All inputs are finite; a program needn't handle non-finite values.
Results may differ from the reference program's by a relative error of at most 0.0058.
Values may be sent and summed in bfloat16 or wider, within the bound.
A program may use at most 64 MiB of HBM per device.

```python
import math
import jax
import jax.numpy as jnp
import numpy as np
from jax import lax

D = 4096
FF = 1024
TOP = 8
EXP_GRP = 4
CAP = 6
COL = 32
EXPERTS = 64
N_BLK = 16
N_MEMBER = 32


def level_of(rng, extent, pieces, least, largest):
    def one(axis_at, blocks):
        draws = jax.random.uniform(jax.random.fold_in(jax.random.fold_in(rng, 6), axis_at), (blocks,), jnp.float32, least / len(pieces), largest / len(pieces))
        return jnp.repeat(jnp.exp(draws), extent[axis_at] // blocks).reshape((-1,) + (1,) * (len(extent) - axis_at - 1))

    gain = one(*pieces[0])
    for cut in pieces[1:]:
        gain = gain * one(*cut)
    return gain


def routed_block(stream_key, own, number, rows, amount, top, reach, skew):
    ranking = jax.random.permutation(stream_key, amount)
    packed, common = load_shares(amount, rows * top, reach, skew, True), load_shares(amount, rows * top, reach, skew, False)
    places = jnp.arange(amount)

    def named(lengths, turn):
        used = int((lengths > 0).sum())
        fixed = max(1, used // 4)
        passed = fixed + (places - fixed + turn * (used - fixed)) % max(1, amount - fixed)
        return jnp.zeros((amount,), jnp.int32).at[ranking[jnp.where(places < fixed, places, passed)]].set(jnp.asarray(lengths, jnp.int32))

    lengths = jnp.where(number % 4 == 0, named(packed, number // 4), named(common, number - number // 4 - 1))
    mixed = jax.random.permutation(jax.random.fold_in(own, 3), amount)
    donor, taker = mixed[0:amount // 2 * 2:2], mixed[1:amount // 2 * 2:2]
    margin = jnp.minimum(lengths[donor] - 1, reach - lengths[taker]) // 2
    margin = jnp.where((donor == ranking[0]) | (taker == ranking[0]) | (lengths[taker] == 0), 0, jnp.maximum(margin, 0))
    passed = jax.random.randint(jax.random.fold_in(own, 4), (amount // 2,), 0, 1 << 20) % (margin + 1)
    lengths = lengths.at[donor].add(-passed).at[taker].add(passed)
    labels = jnp.searchsorted(jnp.cumsum(lengths), jnp.arange(rows * top), side="right").astype(jnp.int32)
    grid = labels.reshape(top, rows).T
    grid = grid[jax.random.permutation(jax.random.fold_in(own, 1), rows)]
    turn = jax.random.randint(jax.random.fold_in(own, 2), (rows, 1), 0, top)
    return jnp.take_along_axis(grid, (jnp.arange(top)[None, :] + turn) % top, axis=1)


def load_shares(number_of, total, limit, slope, full):
    weights = [(1 << 20) // math.isqrt(rank ** slope) + 1 for rank in range(1, number_of + 1)]
    largest = limit if full else min(limit, max(-(-total // number_of), total * weights[0] // sum(weights)))
    least = 1 if total - largest >= number_of - 1 else 0
    counts, spare = [largest] + [least] * (number_of - 1), total - largest - least * (number_of - 1)
    while spare > 0:
        free = [i for i in range(1, number_of) if counts[i] < largest] or [i for i in range(1, number_of) if counts[i] < limit]
        pool, remaining = sum([weights[i] for i in free]), spare
        for i in free:
            extra = min(limit - counts[i], max(1, remaining * weights[i] // pool), spare)
            counts[i] = counts[i] + extra
            spare = spare - extra
    return np.array(counts)


def bell_draw(key, shape, deviation, most, cuts=(), kind=jnp.bfloat16):
    result = deviation * jax.random.normal(key, shape, jnp.float32)
    if cuts:
        result = result * level_of(key, shape, cuts, -0.22, 0.18)
    return jnp.clip(result, -most, most).astype(kind)


def setup_inputs(seed: int = 0) -> dict:
    key_of = jax.random.split(jax.random.key(seed), 8)
    tokens = bell_draw(key_of[0], (N_MEMBER, COL, D), 1.0, 6.0, ((0, 32), (1, 16)))
    cotangent = bell_draw(key_of[1], (N_MEMBER, COL, D), 1.0, 6.0, ((0, 32), (1, 16)))
    routes_keys = jax.random.split(jax.random.fold_in(key_of[2], 1), N_MEMBER * COL // COL)
    routes_turns = jax.random.permutation(jax.random.fold_in(key_of[2], 3), N_MEMBER * COL // COL)
    routes = jax.vmap(lambda own, number: routed_block(jax.random.fold_in(key_of[2], 2), own, number, COL, EXPERTS, TOP, CAP, 2))(routes_keys, routes_turns).reshape((N_MEMBER, COL, TOP))
    gate_wts = jnp.clip(0.2 + 0.8 * jax.random.uniform(key_of[3], (N_MEMBER, COL, TOP), jnp.float32) ** level_of(key_of[3], (N_MEMBER, COL, TOP), ((0, 32),), -0.2, 0.2), 0.2, 1.0)
    w_gate = bell_draw(key_of[4], (N_BLK, EXP_GRP * FF, D), D ** -0.5, 0.09375, ((0, 16), (1, 32)))
    w_up = bell_draw(key_of[5], (N_BLK, EXP_GRP * FF, D), D ** -0.5, 0.09375, ((0, 16), (1, 32)))
    w_down = bell_draw(key_of[6], (N_BLK, EXP_GRP * FF, D), FF ** -0.5, 0.1875, ((0, 16), (1, 32)))
    return dict(tokens=tokens, cotangent=cotangent, routes=routes, gate_wts=gate_wts, w_gate=w_gate, w_up=w_up, w_down=w_down)


def block_sums(pairs, shards, unit_block):
    total = None
    for left, right in pairs:
        lhs = left.astype(jnp.float32).reshape(left.shape[0], shards, unit_block)
        rhs = right.astype(jnp.float32).reshape(shards, unit_block, right.shape[1])
        term = jnp.einsum("rsh,shd->srd", lhs, rhs, precision=lax.Precision.HIGHEST)
        total = term if total is None else total + term
    rounded = lax.optimization_barrier(total.astype(jnp.bfloat16))
    return jnp.sum(rounded.astype(jnp.float32), axis=0)


def reference(tokens, cotangent, routes, gate_wts, w_gate, w_up, w_down):
    members = tokens.shape[0]
    column = tokens.shape[1]
    model_width = tokens.shape[2]
    experts = EXP_GRP * N_BLK
    shards = N_MEMBER // EXP_GRP
    unit_block = FF // shards
    expert_ids = jnp.arange(experts, dtype=jnp.int32)
    matches = (routes[:, :, :, None] == expert_ids[None, None, None, :]).astype(jnp.int32)
    running = jnp.cumsum(matches.reshape(members, column * TOP, experts), axis=1).reshape(matches.shape) - 1
    slot_ids = jnp.sum(matches * running, axis=3).astype(jnp.int32)
    positions = jnp.broadcast_to(jnp.arange(column, dtype=jnp.int32)[None, :, None], routes.shape)
    column_ids = jnp.broadcast_to(jnp.arange(members, dtype=jnp.int32)[:, None, None], routes.shape)
    index_tab = jnp.full((experts, members, CAP), column, dtype=jnp.int32)
    index_tab = index_tab.at[routes, column_ids, slot_ids].set(positions)
    weight_tab = jnp.zeros((experts, members, CAP), dtype=jnp.float32)
    weight_tab = weight_tab.at[routes, column_ids, slot_ids].set(gate_wts)
    zero_row = jnp.zeros((members, 1, model_width), dtype=tokens.dtype)
    padded_x = jnp.concatenate([tokens, zero_row], axis=1)
    padded_g = jnp.concatenate([cotangent, zero_row], axis=1)
    gate_all = w_gate.reshape(experts, FF, model_width)
    up_all = w_up.reshape(experts, FF, model_width)
    down_all = w_down.reshape(experts, FF, model_width)
    member_rows = jnp.arange(members, dtype=jnp.int32)[:, None]

    def one_expert(carry, inputs):
        acc_out, acc_grad = carry
        index_e, weight_e, gate_e, up_e, down_e = inputs
        row_x = padded_x[member_rows, index_e].reshape(members * CAP, model_width)
        row_g = padded_g[member_rows, index_e].reshape(members * CAP, model_width)
        pre_gate = jnp.dot(row_x, gate_e.T, preferred_element_type=jnp.float32)
        pre_up = jnp.dot(row_x, up_e.T, preferred_element_type=jnp.float32)
        logistic = jax.nn.sigmoid(pre_gate)
        activated = pre_gate * logistic
        hidden = (activated * pre_up).astype(jnp.bfloat16)
        out_sum = block_sums([(hidden, down_e)], shards, unit_block)
        d_hidden = jnp.dot(row_g, down_e.T, preferred_element_type=jnp.float32)
        grad_gate = (d_hidden * pre_up * logistic * (1.0 + pre_gate * (1.0 - logistic))).astype(jnp.bfloat16)
        grad_up = (d_hidden * activated).astype(jnp.bfloat16)
        grad_sum = block_sums([(grad_gate, gate_e), (grad_up, up_e)], shards, unit_block)
        scale = weight_e.reshape(members * CAP, 1)
        acc_out = acc_out.at[member_rows, index_e].add((scale * out_sum).reshape(members, CAP, model_width))
        acc_grad = acc_grad.at[member_rows, index_e].add((scale * grad_sum).reshape(members, CAP, model_width))
        return (acc_out, acc_grad), None

    start = jnp.zeros((members, column + 1, model_width), dtype=jnp.float32)
    (acc_out, acc_grad), _ = lax.scan(one_expert, (start, start), (index_tab, weight_tab, gate_all, up_all, down_all))
    layer_out = acc_out[:, :column].astype(jnp.bfloat16)
    grad_in = acc_grad[:, :column].astype(jnp.bfloat16)
    return (layer_out, grad_in)
```

```python
import functools

import jax
import jax.numpy as jnp
import numpy as np
from jax import lax
from jax.experimental import pallas as pl
from jax.experimental.pallas import tpu as pltpu
from jax.sharding import PartitionSpec as P

MESH = pl.DeviceIdType.MESH
EXP_GRP = 4
CAP = 6
PAD = 8
SHARDS = 8
COLS = 32
BLKS = 16
BF = jnp.bfloat16
F32 = jnp.float32
NT = (((1,), (1,)), ((), ()))
VMEM_SPEC = pl.BlockSpec(memory_space=pltpu.VMEM)
CHUNKS = 4


def loop(start, stop, step):
    def run(k, carry):
        step(k)
        return carry

    lax.fori_loop(start, stop, run, 0)


def greet(axis, me, n):
    barrier = pltpu.get_barrier_semaphore()
    loop(
        1,
        n,
        lambda k: pl.semaphore_signal(
            barrier, inc=1, device_id={axis: lax.rem(me + k, n)}, device_id_type=MESH
        ),
    )
    pl.semaphore_wait(barrier, n - 1)


def send(src, dst, send_sem, recv_sem, axis, peer):
    return pltpu.make_async_remote_copy(
        src_ref=src,
        dst_ref=dst,
        send_sem=send_sem,
        recv_sem=recv_sem,
        device_id={axis: peer},
        device_id_type=MESH,
    )


def flip(m, w):
    return m + w - 2 * w * lax.rem(m // w, 2)


def gather_kernel(x, g, out, send_sem, recv_sem):
    me = lax.axis_index("blk")
    greet("blk", me, BLKS)

    def copies(k):
        peer = lax.rem(me + k, BLKS)
        return [
            send(src.at[0], out.at[me, h], send_sem.at[h, k], recv_sem.at[h, k], "blk", peer)
            for h, src in enumerate((x, g))
        ]

    loop(1, BLKS, lambda k: [c.start() for c in copies(k)])
    out[me, 0] = x[0]
    out[me, 1] = g[0]
    loop(1, BLKS, lambda k: [c.wait() for c in copies(k)])


def swap_kernel(src, out, send_sem, recv_sem):
    me = lax.axis_index("blk")
    greet("blk", me, BLKS)

    def copy(k):
        peer = lax.rem(me + k, BLKS)
        return send(src.at[peer], out.at[me], send_sem.at[k], recv_sem.at[k], "blk", peer)

    loop(1, BLKS, lambda k: copy(k).start())
    out[me] = src[me]
    loop(1, BLKS, lambda k: copy(k).wait())


def dispatch_kernel(src, out, send_sem, recv_sem, own_sem, hop_send, hop_recv):
    me = lax.axis_index("member")
    width = src.shape[1] // SHARDS
    rows = 2 * PAD
    mine = lax.rem(me, SHARDS)
    greet("member", me, COLS)

    def piece(peer):
        return src.at[
            pl.ds(pl.multiple_of(rows * (peer // SHARDS), rows), rows),
            pl.ds(pl.multiple_of(width * lax.rem(peer, SHARDS), width), width),
        ]

    def place(col, part):
        return out.at[
            pl.ds(pl.multiple_of(rows * col, rows), rows),
            pl.ds(pl.multiple_of(width * part, width), width),
        ]

    def put(k):
        peer = lax.rem(me + k, COLS)
        return send(
            piece(peer),
            place(me, lax.rem(peer, SHARDS)),
            send_sem.at[k],
            recv_sem.at[me],
            "member",
            peer,
        )

    own = pltpu.make_async_copy(piece(me), place(me, mine), own_sem)
    loop(1, COLS, lambda k: put(k).start())
    own.start()

    per = COLS // CHUNKS
    tall = rows * per

    def hop(kind, q, origin, peer):
        part = out.at[
            pl.ds(tall * q, tall), pl.ds(pl.multiple_of(width * origin, width), width)
        ]
        return send(part, part, hop_send.at[kind, q], hop_recv.at[kind, q], "member", peer)

    across, along, other = flip(me, 2), flip(me, 4), flip(me, 1)
    part_x, part_y = flip(mine, 2), flip(mine, 4)
    part_xy = flip(part_x, 4)

    def arrived(c):
        @pl.when(c != me)
        def _():
            send(
                place(c, mine), place(c, mine), send_sem.at[0], recv_sem.at[c], "member", other
            ).wait_recv()

    own.wait()
    to_x = [hop(0, q, mine, across) for q in range(CHUNKS)]
    to_y = [hop(1, q, mine, along) for q in range(CHUNKS)]
    pass_y = [hop(2, q, part_x, along) for q in range(CHUNKS)]
    core = [
        [hop(3 + i, q, origin, other) for q in range(CHUNKS)]
        for i, origin in enumerate((mine, part_x, part_y, part_xy))
    ]
    for q in range(CHUNKS):
        loop(per * q, per * (q + 1), arrived)
        to_x[q].start()
        to_y[q].start()
        core[0][q].start()
    for q in range(CHUNKS):
        to_x[q].wait_recv()
        pass_y[q].start()
        core[1][q].start()
    for q in range(CHUNKS):
        to_y[q].wait_recv()
        core[2][q].start()
    for q in range(CHUNKS):
        pass_y[q].wait_recv()
        core[3][q].start()
    loop(1, COLS, lambda k: put(k).wait_send())
    for q in range(CHUNKS):
        for c in (to_x[q], to_y[q], pass_y[q]):
            c.wait_send()
        for i in range(4):
            core[i][q].wait()


def expert_kernel(rows_ref, gate, up, down, pack_o, pack_g, out, acc):
    depth = 512

    acc[...] = jnp.zeros_like(acc)

    def first(k, carry):
        cols = pl.ds(pl.multiple_of(depth * k, depth), depth)
        left = rows_ref[:, cols]
        for i, w in enumerate((gate, up, down)):
            acc[i] += lax.dot_general(left, w[:, cols], NT, preferred_element_type=F32)
        return carry

    lax.fori_loop(0, rows_ref.shape[1] // depth, first, 0)
    n = gate.shape[0]
    split = [acc[i].reshape(COLS, 2, PAD, n) for i in range(3)]
    pre_gate = split[0][:, 0].reshape(COLS * PAD, n)
    pre_up = split[1][:, 0].reshape(COLS * PAD, n)
    d_hidden = split[2][:, 1].reshape(COLS * PAD, n)
    logistic = jax.nn.sigmoid(pre_gate)
    activated = pre_gate * logistic
    hidden = (activated * pre_up).astype(BF)
    grad_gate = (d_hidden * pre_up * logistic * (1.0 + pre_gate * (1.0 - logistic))).astype(BF)
    grad_up = (d_hidden * activated).astype(BF)
    lhs_d = jnp.dot(pack_o[...], hidden, preferred_element_type=F32).astype(BF)
    lhs_g = jnp.dot(pack_g[...], grad_gate, preferred_element_type=F32).astype(BF)
    lhs_u = jnp.dot(pack_g[...], grad_up, preferred_element_type=F32).astype(BF)

    def second(k, carry):
        cols = pl.ds(pl.multiple_of(depth * k, depth), depth)
        total = jnp.dot(lhs_d, down[:, cols], preferred_element_type=F32)
        total += jnp.dot(lhs_g, gate[:, cols], preferred_element_type=F32)
        total += jnp.dot(lhs_u, up[:, cols], preferred_element_type=F32)
        out[:, cols] = total.astype(BF)
        return carry

    lax.fori_loop(0, rows_ref.shape[1] // depth, second, 0)


def collect_kernel(
    og, unpack, out, t1, s1, t2, s2, t3, home, c_send, c_recv, y_send, y_recv, x_send, x_recv,
    h_send, h_recv, own_sem,
):
    me = lax.axis_index("member")
    width = og.shape[1] // SHARDS
    mine = lax.rem(me, SHARDS)
    bit_c, bit_x, bit_y = lax.rem(me, 2), lax.rem(me // 2, 2), lax.rem(me // 4, 2)
    across, along, other = flip(me, 2), flip(me, 4), flip(me, 1)
    tall = og.shape[0] // CHUNKS
    per = COLS // CHUNKS
    rows = 2 * PAD
    greet("member", me, COLS)

    def span(q):
        return pl.ds(tall * q, tall)

    def lanes(part):
        return pl.ds(pl.multiple_of(width * part, width), width)

    def swap_core(q, h):
        return send(
            og.at[span(q), lanes(2 * h + 1 - bit_c)],
            t1.at[h, span(q)],
            c_send.at[q, h],
            c_recv.at[q, h],
            "member",
            other,
        )

    def swap_y(q, i):
        return send(
            s1.at[2 * (1 - bit_y) + i, span(q)],
            t2.at[i, span(q)],
            y_send.at[q, i],
            y_recv.at[q, i],
            "member",
            along,
        )

    def swap_x(q):
        return send(
            s2.at[1 - bit_x, span(q)], t3.at[span(q)], x_send.at[q], x_recv.at[q], "member", across
        )

    def spot(source):
        return out.at[
            pl.ds(pl.multiple_of(rows * (source // SHARDS), rows), rows),
            lanes(lax.rem(source, SHARDS)),
        ]

    def deliver(c):
        return send(
            home.at[pl.ds(pl.multiple_of(rows * c, rows), rows)],
            spot(me),
            h_send.at[c],
            h_recv.at[me],
            "member",
            c,
        )

    def others(step):
        def run(c):
            @pl.when(c != me)
            def _():
                step(c)

        return run

    for q in range(CHUNKS):
        for h in range(4):
            swap_core(q, h).start()
    for q in range(CHUNKS):
        for h in range(4):
            swap_core(q, h).wait_recv()
            total = og[span(q), lanes(2 * h + bit_c)].astype(F32) + t1[h, span(q)].astype(F32)
            s1[h, span(q)] = total.astype(BF)
        for i in range(2):
            swap_y(q, i).start()
    for q in range(CHUNKS):
        for i in range(2):
            swap_y(q, i).wait_recv()
            total = s1[2 * bit_y + i, span(q)].astype(F32) + t2[i, span(q)].astype(F32)
            s2[i, span(q)] = total.astype(BF)
        swap_x(q).start()
    for q in range(CHUNKS):
        swap_x(q).wait_recv()
        total = s2[bit_x, span(q)].astype(F32) + t3[span(q)].astype(F32)
        wide = jnp.dot(unpack[...], total.astype(BF), preferred_element_type=F32)
        home[pl.ds(rows * per * q, rows * per)] = wide.astype(BF)
        loop(per * q, per * (q + 1), others(lambda c: deliver(c).start()))
    own = pltpu.make_async_copy(
        home.at[pl.ds(pl.multiple_of(rows * me, rows), rows)], spot(me), own_sem
    )
    own.start()
    for q in range(CHUNKS):
        for h in range(4):
            swap_core(q, h).wait_send()
        for i in range(2):
            swap_y(q, i).wait_send()
        swap_x(q).wait_send()
    loop(0, COLS, others(lambda c: deliver(c).wait_send()))

    def landed(c):
        send(
            home.at[pl.ds(0, rows)], spot(c), h_send.at[0], h_recv.at[c], "member", other
        ).wait_recv()

    loop(0, COLS, others(landed))
    own.wait()


def remote_call(kernel, n_in, shape, scratch, ident):
    return pl.pallas_call(
        kernel,
        out_shape=jax.ShapeDtypeStruct(shape, BF),
        in_specs=[VMEM_SPEC] * n_in,
        out_specs=VMEM_SPEC,
        scratch_shapes=scratch,
        compiler_params=pltpu.CompilerParams(collective_id=ident, has_side_effects=True),
    )


def packing():
    pack = np.zeros((2, COLS * 2 * CAP, COLS * PAD), np.float32)
    unpack = np.zeros((COLS // CHUNKS * 2 * PAD, COLS // CHUNKS * 2 * CAP), np.float32)
    for c in range(COLS):
        for h in range(2):
            for r in range(CAP):
                pack[h, (c * 2 + h) * CAP + r, c * PAD + r] = 1
                if c < COLS // CHUNKS:
                    unpack[(c * 2 + h) * PAD + r, (c * 2 + h) * CAP + r] = 1
    return jnp.asarray(pack[0], BF), jnp.asarray(pack[1], BF), jnp.asarray(unpack, BF)


def body(tokens, cotangent, routes, gate_wts, w_gate, w_up, w_down):
    width = tokens.shape[2]
    dma = pltpu.SemaphoreType.DMA
    pack_o, pack_g, unpack = packing()

    experts = lax.axis_index("blk") * EXP_GRP + jnp.arange(EXP_GRP, dtype=jnp.int32)
    match = routes[0][None] == experts[:, None, None]
    named = jnp.sum(match.astype(F32), axis=2)
    weight = jnp.sum(jnp.where(match, gate_wts[0][None], 0.0), axis=2)
    earlier = np.tril(np.ones((COLS, COLS), np.float32), -1)
    rank = jnp.sum(named[:, None, :] * earlier[None], axis=2)
    places = jnp.arange(PAD, dtype=jnp.int32).astype(F32)
    taken = jnp.where(
        (rank[:, None, :] == places[None, :, None]) & (named[:, None, :] > 0), 1.0, 0.0
    )
    both = np.eye(2, dtype=np.float32)[None, :, None, None, :, None]

    def table(values):
        grid = values.reshape(EXP_GRP, 1, PAD, BLKS, 1, COLS // BLKS) * both
        return grid.reshape(EXP_GRP * 2 * PAD, 2 * COLS)

    picker = table(taken).astype(BF)
    combine = table(taken * weight[:, None, :]).T

    column = remote_call(
        gather_kernel,
        2,
        (BLKS, 2, COLS // BLKS, width),
        [dma((2, BLKS)), dma((2, BLKS))],
        0,
    )(tokens, cotangent)
    picked = jnp.dot(
        picker, column.reshape(2 * COLS, width), preferred_element_type=F32
    ).astype(BF)
    arrived = remote_call(
        dispatch_kernel,
        1,
        (COLS * 2 * PAD, width),
        [dma((COLS,)), dma((COLS,)), dma(()), dma((7, CHUNKS)), dma((7, CHUNKS))],
        1,
    )(picked)
    part = pl.pallas_call(
        expert_kernel,
        out_shape=jax.ShapeDtypeStruct((COLS * 2 * CAP, width), BF),
        in_specs=[VMEM_SPEC] * 6,
        out_specs=VMEM_SPEC,
        scratch_shapes=[pltpu.VMEM((3, COLS * 2 * PAD, w_gate.shape[1]), F32)],
    )(arrived, w_gate[0], w_up[0], w_down[0], pack_o, pack_g)
    dense, piece = COLS * 2 * CAP, width // SHARDS
    sums = remote_call(
        collect_kernel,
        2,
        (EXP_GRP * 2 * PAD, width),
        [
            pltpu.VMEM((4, dense, piece), BF),
            pltpu.VMEM((4, dense, piece), BF),
            pltpu.VMEM((2, dense, piece), BF),
            pltpu.VMEM((2, dense, piece), BF),
            pltpu.VMEM((dense, piece), BF),
            pltpu.VMEM((COLS * 2 * PAD, piece), BF),
            dma((CHUNKS, 4)),
            dma((CHUNKS, 4)),
            dma((CHUNKS, 2)),
            dma((CHUNKS, 2)),
            dma((CHUNKS,)),
            dma((CHUNKS,)),
            dma((COLS,)),
            dma((COLS,)),
            dma(()),
        ],
        2,
    )(part, unpack)
    mixed = jnp.dot(
        combine, sums.astype(F32), precision=lax.Precision.HIGHEST, preferred_element_type=F32
    ).astype(BF)
    shares = remote_call(
        swap_kernel,
        1,
        (BLKS, 2, COLS // BLKS, width),
        [dma((BLKS,)), dma((BLKS,))],
        3,
    )(mixed.reshape(BLKS, 2, COLS // BLKS, width))
    final = jnp.sum(shares.astype(F32), axis=0).astype(BF)
    return final[0][None], final[1][None]


def solution(mesh):
    placed = (
        P("member", "blk", None),
        P("member", "blk", None),
        P("member", None, None),
        P("member", None, None),
        P("blk", "member", None),
        P("blk", "member", None),
        P("blk", "member", None),
    )
    return jax.shard_map(
        body,
        mesh=mesh,
        in_specs=placed,
        out_specs=(P("member", "blk", None), P("member", "blk", None)),
        check_vma=False,
    )
```

```python
import jax
import jax.numpy as jnp
import numpy as np
from jax import lax
from jax.experimental import pallas as pl
from jax.experimental.pallas import tpu as pltpu
from jax.sharding import PartitionSpec as P

MESH = pl.DeviceIdType.MESH
EXP_GRP = 4
CAP = 6
PAD = 8
SHARDS = 8
COLS = 32
BLKS = 16
BF = jnp.bfloat16
F32 = jnp.float32
NT = (((1,), (1,)), ((), ()))
VMEM_SPEC = pl.BlockSpec(memory_space=pltpu.VMEM)
CHUNKS = 4


def loop(start, stop, step):
    def run(k, carry):
        step(k)
        return carry

    lax.fori_loop(start, stop, run, 0)


def greet(axis, me, n):
    barrier = pltpu.get_barrier_semaphore()
    loop(
        1,
        n,
        lambda k: pl.semaphore_signal(
            barrier, inc=1, device_id={axis: lax.rem(me + k, n)}, device_id_type=MESH
        ),
    )
    pl.semaphore_wait(barrier, n - 1)


def send(src, dst, send_sem, recv_sem, axis, peer):
    return pltpu.make_async_remote_copy(
        src_ref=src,
        dst_ref=dst,
        send_sem=send_sem,
        recv_sem=recv_sem,
        device_id={axis: peer},
        device_id_type=MESH,
    )


def flip(m, w):
    return m + w - 2 * w * lax.rem(m // w, 2)


def greet_few(axis, peers):
    barrier = pltpu.get_barrier_semaphore()
    for peer in peers:
        pl.semaphore_signal(barrier, inc=1, device_id={axis: peer}, device_id_type=MESH)
    pl.semaphore_wait(barrier, len(peers))


FAR_FIRST = (4, 3, 5, 2, 6, 1, 7)
NEAR_FIRST = (1, 7, 2, 6, 3, 5, 4)


def gather_kernel(x, g, out, send_sem, recv_sem, pass_send, pass_recv):
    me = lax.axis_index("blk")
    partner = flip(me, 1)
    ahead = {k: lax.rem(me + 2 * k, BLKS) for k in range(1, 8)}
    greet_few("blk", [ahead[k] for k in FAR_FIRST] + [partner])

    def first(k, peer):
        return [
            send(src.at[0], out.at[me, h], send_sem.at[h, k], recv_sem.at[h, k], "blk", peer)
            for h, src in enumerate((x, g))
        ]

    def passed(k, source):
        return send(
            out.at[source], out.at[source], pass_send.at[k], pass_recv.at[k], "blk", partner
        )

    direct = {k: first(k, ahead[k]) for k in FAR_FIRST}
    direct[0] = first(0, partner)
    for k in FAR_FIRST + (0,):
        for c in direct[k]:
            c.start()
    out[me, 0] = x[0]
    out[me, 1] = g[0]
    relays = []
    for k in NEAR_FIRST:
        for c in direct[k]:
            c.wait_recv()
        relay = passed(k, lax.rem(me + BLKS - 2 * k, BLKS))
        relay.start()
        relays.append(relay)
    for c in direct[0]:
        c.wait_recv()
    for k in FAR_FIRST + (0,):
        for c in direct[k]:
            c.wait_send()
    for relay in relays:
        relay.wait()


def swap_kernel(src, out_a, out_b, near, mid, far, send_sem, recv_sem, far_send, far_recv):
    me = lax.axis_index("blk")
    partner = flip(me, 1)
    ahead = {k: lax.rem(me + 2 * k, BLKS) for k in range(8)}
    greet_few("blk", [ahead[k] for k in FAR_FIRST] + [partner])

    def pair(k):
        return send(
            src.at[flip(ahead[k], 1)],
            near.at[flip(ahead[k], 1) // 2],
            send_sem.at[k],
            recv_sem.at[k],
            "blk",
            partner,
        )

    def along(k):
        return send(mid.at[k], far.at[k], far_send.at[k], far_recv.at[k], "blk", ahead[k])

    order = FAR_FIRST + (0,)
    for k in order:
        pair(k).start()
    for k in order:
        pair(k).wait_recv()
        total = src[ahead[k]].astype(F32) + near[ahead[k] // 2].astype(F32)
        if k:
            mid[k] = total.astype(BF)
            along(k).start()
    for k in NEAR_FIRST:
        along(k).wait_recv()
        total = total + far[k].astype(F32)
    out_a[0] = total[0].astype(BF)
    out_b[0] = total[1].astype(BF)
    for k in order:
        pair(k).wait_send()
        if k:
            along(k).wait_send()


def layer_kernel(
    src, gate, up, down, pack, unpack, out,
    rows_ref, w, acc, og, t1, s1, t2, s2, t3, home,
    send_sem, recv_sem, own_sem, w_sem, hop_send, hop_recv,
    c_send, c_recv, y_send, y_recv, x_send, x_recv, h_send, h_recv,
):
    me = lax.axis_index("member")
    width = src.shape[1] // SHARDS
    rows = 2 * PAD
    dense = 2 * CAP
    per = COLS // CHUNKS
    mine = lax.rem(me, SHARDS)
    bit_c, bit_x, bit_y = lax.rem(me, 2), lax.rem(me // 2, 2), lax.rem(me // 4, 2)
    across, along, other = flip(me, 2), flip(me, 4), flip(me, 1)
    part_x, part_y = flip(mine, 2), flip(mine, 4)
    part_xy = flip(part_x, 4)

    loads = [
        pltpu.make_async_copy(ref.at[0], w.at[i], w_sem.at[i])
        for i, ref in enumerate((gate, up, down))
    ]
    for load in loads:
        load.start()
    greet("member", me, COLS)

    def some(size, at):
        return pl.ds(pl.multiple_of(size * at, size), size)

    def lanes(part):
        return some(width, part)

    def piece(peer):
        return src.at[some(rows, peer // SHARDS), lanes(lax.rem(peer, SHARDS))]

    def place(col, part):
        return rows_ref.at[some(rows, col), lanes(part)]

    def put(k):
        peer = lax.rem(me + k, COLS)
        return send(
            piece(peer),
            place(me, lax.rem(peer, SHARDS)),
            send_sem.at[k],
            recv_sem.at[me],
            "member",
            peer,
        )

    def others(step):
        def run(c):
            @pl.when(c != me)
            def _():
                step(c)

        return run

    def arrived(c):
        send(
            place(c, mine), place(c, mine), send_sem.at[0], recv_sem.at[c], "member", other
        ).wait_recv()

    def hop(kind, q, origin, peer):
        part = rows_ref.at[some(rows * per, q), lanes(origin)]
        return send(part, part, hop_send.at[kind, q], hop_recv.at[kind, q], "member", peer)

    to_x = lambda q: hop(0, q, mine, across)
    to_y = lambda q: hop(1, q, mine, along)
    pass_y = lambda q: hop(2, q, part_x, along)
    origins = (mine, part_x, part_y, part_xy)
    core = lambda i, q: hop(3 + i, q, origins[i], other)

    def multiply(q, origin, fresh=False):
        span, cols = some(rows * per, q), lanes(origin)
        left = rows_ref[span, cols]
        for i in range(3):
            term = lax.dot_general(left, w[i, :, cols], NT, preferred_element_type=F32)
            acc[i, span] = term if fresh else acc[i, span] + term

    own = pltpu.make_async_copy(piece(me), place(me, mine), own_sem.at[0])
    loop(1, COLS, lambda k: put(k).start())
    own.start()
    own.wait()

    def phase_own(q):
        loop(per * q, per * (q + 1), others(arrived))
        to_x(q).start()
        to_y(q).start()
        core(0, q).start()

    def phase_x(q):
        to_x(q).wait_recv()
        pass_y(q).start()
        core(1, q).start()
        multiply(q, part_x)

    def phase_y(q):
        to_y(q).wait_recv()
        core(2, q).start()
        multiply(q, part_y)

    def phase_core(q):
        for i in range(3):
            core(i, q).wait_recv()
            multiply(q, flip(origins[i], 1))

    def swap_core(q, h):
        return send(
            og.at[some(dense * per, q), lanes(2 * h + 1 - bit_c)],
            t1.at[h, some(dense * per, q)],
            c_send.at[q, h],
            c_recv.at[q, h],
            "member",
            other,
        )

    def finish(q):
        pass_y(q).wait_recv()
        core(3, q).start()
        multiply(q, part_xy)
        core(3, q).wait_recv()
        multiply(q, flip(part_xy, 1))
        n = w.shape[1]
        split = [acc[i, some(rows * per, q)].reshape(per, 2, PAD, n) for i in range(3)]
        pre_gate = split[0][:, 0].reshape(per * PAD, n)
        pre_up = split[1][:, 0].reshape(per * PAD, n)
        d_hidden = split[2][:, 1].reshape(per * PAD, n)
        logistic = jax.nn.sigmoid(pre_gate)
        activated = pre_gate * logistic
        hidden = (activated * pre_up).astype(BF)
        grad_gate = (
            d_hidden * pre_up * logistic * (1.0 + pre_gate * (1.0 - logistic))
        ).astype(BF)
        grad_up = (d_hidden * activated).astype(BF)
        left = [
            jnp.dot(pack[h], v, preferred_element_type=F32).astype(BF)
            for h, v in ((1, grad_gate), (1, grad_up), (0, hidden))
        ]

        def second(k):
            cols = lanes(k)
            total = jnp.dot(left[0], w[0, :, cols], preferred_element_type=F32)
            total += jnp.dot(left[1], w[1, :, cols], preferred_element_type=F32)
            total += jnp.dot(left[2], w[2, :, cols], preferred_element_type=F32)
            og[some(dense * per, q), cols] = total.astype(BF)

        loop(0, SHARDS, second)
        for h in range(4):
            swap_core(q, h).start()

    loop(0, CHUNKS, phase_own)
    for load in loads:
        load.wait()
    loop(0, CHUNKS, lambda q: multiply(q, mine, True))
    loop(0, CHUNKS, phase_x)
    loop(0, CHUNKS, phase_y)
    loop(0, CHUNKS, phase_core)
    loop(0, CHUNKS, finish)

    def span(q):
        return some(dense * per, q)

    def swap_y(q, i):
        return send(
            s1.at[2 * (1 - bit_y) + i, span(q)],
            t2.at[i, span(q)],
            y_send.at[q, i],
            y_recv.at[q, i],
            "member",
            along,
        )

    def swap_x(q):
        return send(
            s2.at[1 - bit_x, span(q)], t3.at[span(q)], x_send.at[q], x_recv.at[q], "member", across
        )

    def spot(source):
        return out.at[some(rows, source // SHARDS), lanes(lax.rem(source, SHARDS))]

    def deliver(c):
        return send(
            home.at[some(rows, c)], spot(me), h_send.at[c], h_recv.at[me], "member", c
        )

    def add_core(q):
        for h in range(4):
            swap_core(q, h).wait_recv()
            total = og[span(q), lanes(2 * h + bit_c)].astype(F32) + t1[h, span(q)].astype(F32)
            s1[h, span(q)] = total.astype(BF)
        for i in range(2):
            swap_y(q, i).start()

    def add_y(q):
        for i in range(2):
            swap_y(q, i).wait_recv()
            total = s1[2 * bit_y + i, span(q)].astype(F32) + t2[i, span(q)].astype(F32)
            s2[i, span(q)] = total.astype(BF)
        swap_x(q).start()

    def add_x(q):
        swap_x(q).wait_recv()
        total = s2[bit_x, span(q)].astype(F32) + t3[span(q)].astype(F32)
        wide = jnp.dot(unpack[...], total.astype(BF), preferred_element_type=F32)
        home[some(rows * per, q)] = wide.astype(BF)
        loop(per * q, per * (q + 1), others(lambda c: deliver(c).start()))

    loop(0, CHUNKS, add_core)
    loop(0, CHUNKS, add_y)
    loop(0, CHUNKS, add_x)
    last = pltpu.make_async_copy(home.at[some(rows, me)], spot(me), own_sem.at[1])
    last.start()

    def drain(q):
        to_x(q).wait_send()
        to_y(q).wait_send()
        pass_y(q).wait_send()
        for i in range(4):
            core(i, q).wait_send()
            swap_core(q, i).wait_send()
        for i in range(2):
            swap_y(q, i).wait_send()
        swap_x(q).wait_send()

    def landed(c):
        send(
            home.at[some(rows, 0)], spot(c), h_send.at[0], h_recv.at[c], "member", other
        ).wait_recv()

    loop(1, COLS, lambda k: put(k).wait_send())
    loop(0, CHUNKS, drain)
    loop(0, COLS, others(lambda c: deliver(c).wait_send()))
    loop(0, COLS, others(landed))
    last.wait()


def remote_call(kernel, specs, shape, scratch, ident):
    return pl.pallas_call(
        kernel,
        out_shape=jax.tree.map(lambda dims: jax.ShapeDtypeStruct(dims, BF), shape,
                               is_leaf=lambda v: isinstance(v[0], int)),
        in_specs=specs,
        out_specs=jax.tree.map(lambda dims: VMEM_SPEC, shape,
                               is_leaf=lambda v: isinstance(v[0], int)),
        scratch_shapes=scratch,
        compiler_params=pltpu.CompilerParams(collective_id=ident, has_side_effects=True),
    )


def packing():
    per = COLS // CHUNKS
    pack = np.zeros((2, per * 2 * CAP, per * PAD), np.float32)
    unpack = np.zeros((per * 2 * PAD, per * 2 * CAP), np.float32)
    for c in range(per):
        for h in range(2):
            for r in range(CAP):
                pack[h, (c * 2 + h) * CAP + r, c * PAD + r] = 1
                unpack[(c * 2 + h) * PAD + r, (c * 2 + h) * CAP + r] = 1
    return jnp.asarray(pack, BF), jnp.asarray(unpack, BF)


def body(tokens, cotangent, routes, gate_wts, w_gate, w_up, w_down):
    width = tokens.shape[2]
    dma = pltpu.SemaphoreType.DMA
    pack, unpack = packing()

    experts = lax.axis_index("blk") * EXP_GRP + jnp.arange(EXP_GRP, dtype=jnp.int32)
    match = routes[0][None] == experts[:, None, None]
    named = jnp.sum(match.astype(F32), axis=2)
    weight = jnp.sum(jnp.where(match, gate_wts[0][None], 0.0), axis=2)
    earlier = np.tril(np.ones((COLS, COLS), np.float32), -1)
    rank = jnp.sum(named[:, None, :] * earlier[None], axis=2)
    places = jnp.arange(PAD, dtype=jnp.int32).astype(F32)
    taken = jnp.where(
        (rank[:, None, :] == places[None, :, None]) & (named[:, None, :] > 0), 1.0, 0.0
    )
    both = np.eye(2, dtype=np.float32)[None, :, None, None, :, None]

    def table(values):
        grid = values.reshape(EXP_GRP, 1, PAD, BLKS, 1, COLS // BLKS) * both
        return grid.reshape(EXP_GRP * 2 * PAD, 2 * COLS)

    picker = table(taken).astype(BF)
    combine = table(taken * weight[:, None, :]).T

    pairs = COLS // BLKS
    column = remote_call(
        gather_kernel,
        [VMEM_SPEC] * 2,
        (BLKS, 2, pairs, width),
        [dma((2, 8)), dma((2, 8)), dma((8,)), dma((8,))],
        0,
    )(tokens, cotangent)
    picked = jnp.dot(
        picker, column.reshape(2 * COLS, width), preferred_element_type=F32
    ).astype(BF)
    dense, padded, piece = COLS * 2 * CAP, COLS * 2 * PAD, width // SHARDS
    hidden = w_gate.shape[1]
    sums = remote_call(
        layer_kernel,
        [VMEM_SPEC] + [pl.BlockSpec(memory_space=pl.ANY)] * 3 + [VMEM_SPEC] * 2,
        (EXP_GRP * 2 * PAD, width),
        [
            pltpu.VMEM((padded, width), BF),
            pltpu.VMEM((3, hidden, width), BF),
            pltpu.VMEM((3, padded, hidden), F32),
            pltpu.VMEM((dense, width), BF),
            pltpu.VMEM((4, dense, piece), BF),
            pltpu.VMEM((4, dense, piece), BF),
            pltpu.VMEM((2, dense, piece), BF),
            pltpu.VMEM((2, dense, piece), BF),
            pltpu.VMEM((dense, piece), BF),
            pltpu.VMEM((padded, piece), BF),
            dma((COLS,)),
            dma((COLS,)),
            dma((2,)),
            dma((3,)),
            dma((7, CHUNKS)),
            dma((7, CHUNKS)),
            dma((CHUNKS, 4)),
            dma((CHUNKS, 4)),
            dma((CHUNKS, 2)),
            dma((CHUNKS, 2)),
            dma((CHUNKS,)),
            dma((CHUNKS,)),
            dma((COLS,)),
            dma((COLS,)),
        ],
        1,
    )(picked, w_gate, w_up, w_down, pack, unpack)
    mixed = jnp.dot(
        combine, sums.astype(F32), precision=lax.Precision.HIGHEST, preferred_element_type=F32
    ).astype(BF)
    half = (BLKS // 2, 2, pairs, width)
    return remote_call(
        swap_kernel,
        [VMEM_SPEC],
        ((1, pairs, width), (1, pairs, width)),
        [pltpu.VMEM(half, BF)] * 3 + [dma((8,))] * 4,
        2,
    )(mixed.reshape(BLKS, 2, pairs, width))


def solution(mesh):
    placed = (
        P("member", "blk", None),
        P("member", "blk", None),
        P("member", None, None),
        P("member", None, None),
        P("blk", "member", None),
        P("blk", "member", None),
        P("blk", "member", None),
    )
    return jax.shard_map(
        body,
        mesh=mesh,
        in_specs=placed,
        out_specs=(P("member", "blk", None), P("member", "blk", None)),
        check_vma=False,
    )
```

```python
import jax
import jax.numpy as jnp
import numpy as np
from jax import lax
from jax.experimental import pallas as pl
from jax.experimental.pallas import tpu as pltpu
from jax.sharding import PartitionSpec as P

MESH = pl.DeviceIdType.MESH
EXP_GRP = 4
CAP = 6
PAD = 8
SHARDS = 8
COLS = 32
BLKS = 16
BF = jnp.bfloat16
F32 = jnp.float32
NT = (((1,), (1,)), ((), ()))
VMEM_SPEC = pl.BlockSpec(memory_space=pltpu.VMEM)
CHUNKS = 4


def loop(start, stop, step):
    def run(k, carry):
        step(k)
        return carry

    lax.fori_loop(start, stop, run, 0)


def greet(axis, me, n):
    barrier = pltpu.get_barrier_semaphore()
    loop(
        1,
        n,
        lambda k: pl.semaphore_signal(
            barrier, inc=1, device_id={axis: lax.rem(me + k, n)}, device_id_type=MESH
        ),
    )
    pl.semaphore_wait(barrier, n - 1)


def send(src, dst, send_sem, recv_sem, axis, peer):
    return pltpu.make_async_remote_copy(
        src_ref=src,
        dst_ref=dst,
        send_sem=send_sem,
        recv_sem=recv_sem,
        device_id={axis: peer},
        device_id_type=MESH,
    )


def flip(m, w):
    return m + w - 2 * w * lax.rem(m // w, 2)


def greet_few(axis, peers):
    barrier = pltpu.get_barrier_semaphore()
    for peer in peers:
        pl.semaphore_signal(barrier, inc=1, device_id={axis: peer}, device_id_type=MESH)
    pl.semaphore_wait(barrier, len(peers))


FAR_FIRST = (4, 3, 5, 2, 6, 1, 7)
NEAR_FIRST = (1, 7, 2, 6, 3, 5, 4)


def gather_kernel(x, g, out, send_sem, recv_sem, pass_send, pass_recv):
    me = lax.axis_index("blk")
    partner = flip(me, 1)
    ahead = {k: lax.rem(me + 2 * k, BLKS) for k in range(1, 8)}
    greet_few("blk", [ahead[k] for k in FAR_FIRST] + [partner])

    def first(k, peer):
        return [
            send(src.at[0], out.at[me, h], send_sem.at[h, k], recv_sem.at[h, k], "blk", peer)
            for h, src in enumerate((x, g))
        ]

    def passed(k, source):
        return send(
            out.at[source], out.at[source], pass_send.at[k], pass_recv.at[k], "blk", partner
        )

    direct = {k: first(k, ahead[k]) for k in FAR_FIRST}
    direct[0] = first(0, partner)
    for k in FAR_FIRST + (0,):
        for c in direct[k]:
            c.start()
    out[me, 0] = x[0]
    out[me, 1] = g[0]
    relays = []
    for k in NEAR_FIRST:
        for c in direct[k]:
            c.wait_recv()
        relay = passed(k, lax.rem(me + BLKS - 2 * k, BLKS))
        relay.start()
        relays.append(relay)
    for c in direct[0]:
        c.wait_recv()
    for k in FAR_FIRST + (0,):
        for c in direct[k]:
            c.wait_send()
    for relay in relays:
        relay.wait()


def swap_kernel(src, out_a, out_b, near, mid, far, send_sem, recv_sem, far_send, far_recv):
    me = lax.axis_index("blk")
    partner = flip(me, 1)
    ahead = {k: lax.rem(me + 2 * k, BLKS) for k in range(8)}
    greet_few("blk", [ahead[k] for k in FAR_FIRST] + [partner])

    def pair(k):
        return send(
            src.at[flip(ahead[k], 1)],
            near.at[flip(ahead[k], 1) // 2],
            send_sem.at[k],
            recv_sem.at[k],
            "blk",
            partner,
        )

    def along(k):
        return send(mid.at[k], far.at[k], far_send.at[k], far_recv.at[k], "blk", ahead[k])

    order = FAR_FIRST + (0,)
    for k in order:
        pair(k).start()
    for k in order:
        pair(k).wait_recv()
        total = src[ahead[k]].astype(F32) + near[ahead[k] // 2].astype(F32)
        if k:
            mid[k] = total.astype(BF)
            along(k).start()
    for k in NEAR_FIRST:
        along(k).wait_recv()
        total = total + far[k].astype(F32)
    out_a[0] = total[0].astype(BF)
    out_b[0] = total[1].astype(BF)
    for k in order:
        pair(k).wait_send()
        if k:
            along(k).wait_send()


def layer_kernel(
    src, gate, up, down, pack, unpack, out,
    rows_ref, w, acc, og, t1, s1, t2, s2, t3, home,
    send_sem, recv_sem, own_sem, w_sem, hop_send, hop_recv,
    c_send, c_recv, y_send, y_recv, x_send, x_recv, h_send, h_recv,
):
    me = lax.axis_index("member")
    width = src.shape[1] // SHARDS
    rows = 2 * PAD
    dense = 2 * CAP
    per = COLS // CHUNKS
    mine = lax.rem(me, SHARDS)
    bit_c, bit_x, bit_y = lax.rem(me, 2), lax.rem(me // 2, 2), lax.rem(me // 4, 2)
    across, along, other = flip(me, 2), flip(me, 4), flip(me, 1)
    part_x, part_y = flip(mine, 2), flip(mine, 4)
    part_xy = flip(part_x, 4)

    loads = [
        pltpu.make_async_copy(ref.at[0], w.at[i], w_sem.at[i])
        for i, ref in enumerate((gate, up, down))
    ]
    for load in loads:
        load.start()
    greet("member", me, COLS)

    def some(size, at):
        return pl.ds(pl.multiple_of(size * at, size), size)

    def lanes(part):
        return some(width, part)

    def piece(peer):
        return src.at[some(rows, peer // SHARDS), lanes(lax.rem(peer, SHARDS))]

    def place(col, part):
        return rows_ref.at[some(rows, col), lanes(part)]

    def put(k):
        peer = lax.rem(me + k, COLS)
        return send(
            piece(peer),
            place(me, lax.rem(peer, SHARDS)),
            send_sem.at[k],
            recv_sem.at[me],
            "member",
            peer,
        )

    def others(step):
        def run(c):
            @pl.when(c != me)
            def _():
                step(c)

        return run

    def arrived(c):
        send(
            place(c, mine), place(c, mine), send_sem.at[0], recv_sem.at[c], "member", other
        ).wait_recv()

    def hop(kind, q, origin, peer):
        part = rows_ref.at[some(rows * per, q), lanes(origin)]
        return send(part, part, hop_send.at[kind, q], hop_recv.at[kind, q], "member", peer)

    to_x = lambda q: hop(0, q, mine, across)
    to_y = lambda q: hop(1, q, mine, along)

    def route(q, relay_y, relay_x):
        late = (q + CHUNKS - 1) // CHUNKS
        return (1 - late) * relay_y + late * relay_x

    relay = lambda q: hop(2, q, route(q, part_x, part_y), route(q, along, across))
    origins = (mine, part_x, part_y, part_xy)
    core = lambda i, q: hop(3 + i, q, origins[i], other)

    def multiply(q, origin, fresh=False):
        span, cols = some(rows * per, q), lanes(origin)
        left = rows_ref[span, cols]
        for i in range(3):
            term = lax.dot_general(left, w[i, :, cols], NT, preferred_element_type=F32)
            acc[i, span] = term if fresh else acc[i, span] + term

    own = pltpu.make_async_copy(piece(me), place(me, mine), own_sem.at[0])
    loop(1, COLS, lambda k: put(k).start())
    own.start()
    own.wait()

    def phase_own(q):
        loop(per * q, per * (q + 1), others(arrived))
        to_x(q).start()
        to_y(q).start()
        core(0, q).start()

    def phase_near(q):
        to_x(q).wait_recv()
        core(1, q).start()
        to_y(q).wait_recv()
        relay(q).start()
        core(2, q).start()
        multiply(q, part_x)
        multiply(q, part_y)

    def phase_core(q):
        for i in range(3):
            core(i, q).wait_recv()
            multiply(q, flip(origins[i], 1))

    def swap_core(q, h):
        return send(
            og.at[some(dense * per, q), lanes(2 * h + 1 - bit_c)],
            t1.at[h, some(dense * per, q)],
            c_send.at[q, h],
            c_recv.at[q, h],
            "member",
            other,
        )

    def finish(q):
        relay(q).wait_recv()
        core(3, q).start()
        multiply(q, part_xy)
        core(3, q).wait_recv()
        multiply(q, flip(part_xy, 1))
        n = w.shape[1]
        split = [acc[i, some(rows * per, q)].reshape(per, 2, PAD, n) for i in range(3)]
        pre_gate = split[0][:, 0].reshape(per * PAD, n)
        pre_up = split[1][:, 0].reshape(per * PAD, n)
        d_hidden = split[2][:, 1].reshape(per * PAD, n)
        logistic = jax.nn.sigmoid(pre_gate)
        activated = pre_gate * logistic
        hidden = (activated * pre_up).astype(BF)
        grad_gate = (
            d_hidden * pre_up * logistic * (1.0 + pre_gate * (1.0 - logistic))
        ).astype(BF)
        grad_up = (d_hidden * activated).astype(BF)
        left = [
            jnp.dot(pack[h], v, preferred_element_type=F32).astype(BF)
            for h, v in ((1, grad_gate), (1, grad_up), (0, hidden))
        ]

        def second(k):
            cols = lanes(k)
            total = jnp.dot(left[0], w[0, :, cols], preferred_element_type=F32)
            total += jnp.dot(left[1], w[1, :, cols], preferred_element_type=F32)
            total += jnp.dot(left[2], w[2, :, cols], preferred_element_type=F32)
            og[some(dense * per, q), cols] = total.astype(BF)

        loop(0, SHARDS, second)
        for h in range(4):
            swap_core(q, h).start()

    loop(0, CHUNKS, phase_own)
    for load in loads:
        load.wait()
    loop(0, CHUNKS, lambda q: multiply(q, mine, True))
    loop(0, CHUNKS, phase_near)
    loop(0, CHUNKS, phase_core)
    finish(0)

    def span(q):
        return some(dense * per, q)

    def swap_pair(q, i):
        return send(
            s1.at[route(q, 2 * (1 - bit_y) + i, 2 * i + 1 - bit_x), span(q)],
            t2.at[i, span(q)],
            y_send.at[q, i],
            y_recv.at[q, i],
            "member",
            route(q, along, across),
        )

    def swap_last(q):
        return send(
            s2.at[1 - route(q, bit_x, bit_y), span(q)],
            t3.at[span(q)],
            x_send.at[q],
            x_recv.at[q],
            "member",
            route(q, across, along),
        )

    def spot(source):
        return out.at[some(rows, source // SHARDS), lanes(lax.rem(source, SHARDS))]

    def deliver(c):
        return send(
            home.at[some(rows, c)], spot(me), h_send.at[c], h_recv.at[me], "member", c
        )

    def add_core(q):
        for h in range(4):
            swap_core(q, h).wait_recv()
            total = og[span(q), lanes(2 * h + bit_c)].astype(F32) + t1[h, span(q)].astype(F32)
            s1[h, span(q)] = total.astype(BF)
        for i in range(2):
            swap_pair(q, i).start()

    def add_pair(q):
        for i in range(2):
            swap_pair(q, i).wait_recv()
            kept = s1[route(q, 2 * bit_y + i, 2 * i + bit_x), span(q)]
            s2[i, span(q)] = (kept.astype(F32) + t2[i, span(q)].astype(F32)).astype(BF)
        swap_last(q).start()

    def add_last(q):
        swap_last(q).wait_recv()
        total = s2[route(q, bit_x, bit_y), span(q)].astype(F32) + t3[span(q)].astype(F32)
        wide = jnp.dot(unpack[...], total.astype(BF), preferred_element_type=F32)
        home[some(rows * per, q)] = wide.astype(BF)
        loop(per * q, per * (q + 1), others(lambda c: deliver(c).start()))

    def step(q):
        finish(q)
        add_core(q - 1)

    loop(1, CHUNKS, step)
    add_core(CHUNKS - 1)
    loop(0, CHUNKS, add_pair)
    loop(0, CHUNKS, add_last)
    last = pltpu.make_async_copy(home.at[some(rows, me)], spot(me), own_sem.at[1])
    last.start()

    def drain(q):
        to_x(q).wait_send()
        to_y(q).wait_send()
        relay(q).wait_send()
        for i in range(4):
            core(i, q).wait_send()
            swap_core(q, i).wait_send()
        for i in range(2):
            swap_pair(q, i).wait_send()
        swap_last(q).wait_send()

    def landed(c):
        send(
            home.at[some(rows, 0)], spot(c), h_send.at[0], h_recv.at[c], "member", other
        ).wait_recv()

    loop(1, COLS, lambda k: put(k).wait_send())
    loop(0, CHUNKS, drain)
    loop(0, COLS, others(lambda c: deliver(c).wait_send()))
    loop(0, COLS, others(landed))
    last.wait()


def remote_call(kernel, specs, shape, scratch, ident):
    return pl.pallas_call(
        kernel,
        out_shape=jax.tree.map(lambda dims: jax.ShapeDtypeStruct(dims, BF), shape,
                               is_leaf=lambda v: isinstance(v[0], int)),
        in_specs=specs,
        out_specs=jax.tree.map(lambda dims: VMEM_SPEC, shape,
                               is_leaf=lambda v: isinstance(v[0], int)),
        scratch_shapes=scratch,
        compiler_params=pltpu.CompilerParams(collective_id=ident, has_side_effects=True),
    )


def packing():
    per = COLS // CHUNKS
    pack = np.zeros((2, per * 2 * CAP, per * PAD), np.float32)
    unpack = np.zeros((per * 2 * PAD, per * 2 * CAP), np.float32)
    for c in range(per):
        for h in range(2):
            for r in range(CAP):
                pack[h, (c * 2 + h) * CAP + r, c * PAD + r] = 1
                unpack[(c * 2 + h) * PAD + r, (c * 2 + h) * CAP + r] = 1
    return jnp.asarray(pack, BF), jnp.asarray(unpack, BF)


def body(tokens, cotangent, routes, gate_wts, w_gate, w_up, w_down):
    width = tokens.shape[2]
    dma = pltpu.SemaphoreType.DMA
    pack, unpack = packing()

    experts = lax.axis_index("blk") * EXP_GRP + jnp.arange(EXP_GRP, dtype=jnp.int32)
    match = routes[0][None] == experts[:, None, None]
    named = jnp.sum(match.astype(F32), axis=2)
    weight = jnp.sum(jnp.where(match, gate_wts[0][None], 0.0), axis=2)
    earlier = np.tril(np.ones((COLS, COLS), np.float32), -1)
    rank = jnp.sum(named[:, None, :] * earlier[None], axis=2)
    places = jnp.arange(PAD, dtype=jnp.int32).astype(F32)
    taken = jnp.where(
        (rank[:, None, :] == places[None, :, None]) & (named[:, None, :] > 0), 1.0, 0.0
    )
    both = np.eye(2, dtype=np.float32)[None, :, None, None, :, None]

    def table(values):
        grid = values.reshape(EXP_GRP, 1, PAD, BLKS, 1, COLS // BLKS) * both
        return grid.reshape(EXP_GRP * 2 * PAD, 2 * COLS)

    picker = table(taken).astype(BF)
    combine = table(taken * weight[:, None, :]).T

    pairs = COLS // BLKS
    column = remote_call(
        gather_kernel,
        [VMEM_SPEC] * 2,
        (BLKS, 2, pairs, width),
        [dma((2, 8)), dma((2, 8)), dma((8,)), dma((8,))],
        0,
    )(tokens, cotangent)
    picked = jnp.dot(
        picker, column.reshape(2 * COLS, width), preferred_element_type=F32
    ).astype(BF)
    dense, padded, piece = COLS * 2 * CAP, COLS * 2 * PAD, width // SHARDS
    hidden = w_gate.shape[1]
    sums = remote_call(
        layer_kernel,
        [VMEM_SPEC] + [pl.BlockSpec(memory_space=pl.ANY)] * 3 + [VMEM_SPEC] * 2,
        (EXP_GRP * 2 * PAD, width),
        [
            pltpu.VMEM((padded, width), BF),
            pltpu.VMEM((3, hidden, width), BF),
            pltpu.VMEM((3, padded, hidden), F32),
            pltpu.VMEM((dense, width), BF),
            pltpu.VMEM((4, dense, piece), BF),
            pltpu.VMEM((4, dense, piece), BF),
            pltpu.VMEM((2, dense, piece), BF),
            pltpu.VMEM((2, dense, piece), BF),
            pltpu.VMEM((dense, piece), BF),
            pltpu.VMEM((padded, piece), BF),
            dma((COLS,)),
            dma((COLS,)),
            dma((2,)),
            dma((3,)),
            dma((7, CHUNKS)),
            dma((7, CHUNKS)),
            dma((CHUNKS, 4)),
            dma((CHUNKS, 4)),
            dma((CHUNKS, 2)),
            dma((CHUNKS, 2)),
            dma((CHUNKS,)),
            dma((CHUNKS,)),
            dma((COLS,)),
            dma((COLS,)),
        ],
        1,
    )(picked, w_gate, w_up, w_down, pack, unpack)
    mixed = jnp.dot(
        combine, sums.astype(F32), precision=lax.Precision.HIGHEST, preferred_element_type=F32
    ).astype(BF)
    half = (BLKS // 2, 2, pairs, width)
    return remote_call(
        swap_kernel,
        [VMEM_SPEC],
        ((1, pairs, width), (1, pairs, width)),
        [pltpu.VMEM(half, BF)] * 3 + [dma((8,))] * 4,
        2,
    )(mixed.reshape(BLKS, 2, pairs, width))


def solution(mesh):
    placed = (
        P("member", "blk", None),
        P("member", "blk", None),
        P("member", None, None),
        P("member", None, None),
        P("blk", "member", None),
        P("blk", "member", None),
        P("blk", "member", None),
    )
    return jax.shard_map(
        body,
        mesh=mesh,
        in_specs=placed,
        out_specs=(P("member", "blk", None), P("member", "blk", None)),
        check_vma=False,
    )
```

```python
import jax
import jax.numpy as jnp
import numpy as np
from jax import lax
from jax.experimental import pallas as pl
from jax.experimental.pallas import tpu as pltpu
from jax.sharding import PartitionSpec as P

MESH = pl.DeviceIdType.MESH
EXP_GRP = 4
CAP = 6
PAD = 8
SHARDS = 8
COLS = 32
BLKS = 16
BF = jnp.bfloat16
F32 = jnp.float32
NT = (((1,), (1,)), ((), ()))
VMEM_SPEC = pl.BlockSpec(memory_space=pltpu.VMEM)
CHUNKS = 4


def loop(start, stop, step):
    def run(k, carry):
        step(k)
        return carry

    lax.fori_loop(start, stop, run, 0)


def greet(axis, me, n):
    barrier = pltpu.get_barrier_semaphore()
    loop(
        1,
        n,
        lambda k: pl.semaphore_signal(
            barrier, inc=1, device_id={axis: lax.rem(me + k, n)}, device_id_type=MESH
        ),
    )
    pl.semaphore_wait(barrier, n - 1)


def send(src, dst, send_sem, recv_sem, axis, peer):
    return pltpu.make_async_remote_copy(
        src_ref=src,
        dst_ref=dst,
        send_sem=send_sem,
        recv_sem=recv_sem,
        device_id={axis: peer},
        device_id_type=MESH,
    )


def flip(m, w):
    return m + w - 2 * w * lax.rem(m // w, 2)


def greet_few(axis, peers):
    barrier = pltpu.get_barrier_semaphore()
    for peer in peers:
        pl.semaphore_signal(barrier, inc=1, device_id={axis: peer}, device_id_type=MESH)
    pl.semaphore_wait(barrier, len(peers))


FAR_FIRST = (4, 3, 5, 2, 6, 1, 7)
NEAR_FIRST = (1, 7, 2, 6, 3, 5, 4)


def gather_kernel(x, g, out, send_sem, recv_sem, pass_send, pass_recv):
    me = lax.axis_index("blk")
    partner = flip(me, 1)
    ahead = {k: lax.rem(me + 2 * k, BLKS) for k in range(1, 8)}
    greet_few("blk", [ahead[k] for k in FAR_FIRST] + [partner])

    def first(k, peer):
        return [
            send(src.at[0], out.at[me, h], send_sem.at[h, k], recv_sem.at[h, k], "blk", peer)
            for h, src in enumerate((x, g))
        ]

    def passed(k, source):
        return send(
            out.at[source], out.at[source], pass_send.at[k], pass_recv.at[k], "blk", partner
        )

    direct = {k: first(k, ahead[k]) for k in FAR_FIRST}
    direct[0] = first(0, partner)
    for k in FAR_FIRST + (0,):
        for c in direct[k]:
            c.start()
    out[me, 0] = x[0]
    out[me, 1] = g[0]
    relays = []
    for k in NEAR_FIRST:
        for c in direct[k]:
            c.wait_recv()
        relay = passed(k, lax.rem(me + BLKS - 2 * k, BLKS))
        relay.start()
        relays.append(relay)
    for c in direct[0]:
        c.wait_recv()
    for k in FAR_FIRST + (0,):
        for c in direct[k]:
            c.wait_send()
    for relay in relays:
        relay.wait()


def swap_kernel(src, out_a, out_b, near, mid, far, send_sem, recv_sem, far_send, far_recv):
    me = lax.axis_index("blk")
    partner = flip(me, 1)
    ahead = {k: lax.rem(me + 2 * k, BLKS) for k in range(8)}
    greet_few("blk", [ahead[k] for k in FAR_FIRST] + [partner])

    def pair(k):
        return send(
            src.at[flip(ahead[k], 1)],
            near.at[flip(ahead[k], 1) // 2],
            send_sem.at[k],
            recv_sem.at[k],
            "blk",
            partner,
        )

    def along(k):
        return send(mid.at[k], far.at[k], far_send.at[k], far_recv.at[k], "blk", ahead[k])

    order = FAR_FIRST + (0,)
    for k in order:
        pair(k).start()
    for k in order:
        pair(k).wait_recv()
        total = src[ahead[k]].astype(F32) + near[ahead[k] // 2].astype(F32)
        if k:
            mid[k] = total.astype(BF)
            along(k).start()
    for k in NEAR_FIRST:
        along(k).wait_recv()
        total = total + far[k].astype(F32)
    out_a[0] = total[0].astype(BF)
    out_b[0] = total[1].astype(BF)
    for k in order:
        pair(k).wait_send()
        if k:
            along(k).wait_send()


def layer_kernel(
    src, gate, up, down, pack, unpack, out,
    rows_ref, w, acc, og, t1, s1, t2, s2, t3, home,
    send_sem, recv_sem, own_sem, w_sem, hop_send, hop_recv,
    c_send, c_recv, y_send, y_recv, x_send, x_recv, h_send, h_recv,
):
    me = lax.axis_index("member")
    width = src.shape[1] // SHARDS
    rows = 2 * PAD
    dense = 2 * CAP
    per = COLS // CHUNKS
    mine = lax.rem(me, SHARDS)
    bit_c, bit_x, bit_y = lax.rem(me, 2), lax.rem(me // 2, 2), lax.rem(me // 4, 2)
    across, along, other = flip(me, 2), flip(me, 4), flip(me, 1)
    part_x, part_y = flip(mine, 2), flip(mine, 4)
    part_xy = flip(part_x, 4)

    loads = [
        pltpu.make_async_copy(ref.at[0], w.at[i], w_sem.at[i])
        for i, ref in enumerate((gate, up, down))
    ]
    for load in loads:
        load.start()
    greet("member", me, COLS)

    def some(size, at):
        return pl.ds(pl.multiple_of(size * at, size), size)

    def lanes(part):
        return some(width, part)

    def piece(peer):
        return src.at[some(rows, peer // SHARDS), lanes(lax.rem(peer, SHARDS))]

    def place(col, part):
        return rows_ref.at[some(rows, col), lanes(part)]

    slot = me // SHARDS

    def chunk(q):
        return lax.rem(slot + q + (q // 2) * (1 - 2 * (q % 2)), CHUNKS)

    def column(q, j):
        return per * chunk(q) + j

    def put(k):
        peer = column(k // per, lax.rem(mine + k, per))
        return send(
            piece(peer),
            place(me, lax.rem(peer, SHARDS)),
            send_sem.at[k],
            recv_sem.at[me],
            "member",
            peer,
        )

    def others(step):
        def run(c):
            @pl.when(c != me)
            def _():
                step(c)

        return run

    def arrived(c):
        send(
            place(c, mine), place(c, mine), send_sem.at[0], recv_sem.at[c], "member", other
        ).wait_recv()

    def hop(kind, q, origin, peer):
        part = rows_ref.at[some(rows * per, chunk(q)), lanes(origin)]
        return send(part, part, hop_send.at[kind, q], hop_recv.at[kind, q], "member", peer)

    to_x = lambda q: hop(0, q, mine, across)
    to_y = lambda q: hop(1, q, mine, along)

    def route(q, relay_y, relay_x):
        late = (q + CHUNKS - 1) // CHUNKS
        return (1 - late) * relay_y + late * relay_x

    relay = lambda q: hop(2, q, route(q, part_x, part_y), route(q, along, across))
    origins = (mine, part_x, part_y, part_xy)
    core = lambda i, q: hop(3 + i, q, origins[i], other)

    def multiply(q, origin, fresh=False):
        span, cols = some(rows * per, q), lanes(origin)
        left = rows_ref[some(rows * per, chunk(q)), cols]
        for i in range(3):
            term = lax.dot_general(left, w[i, :, cols], NT, preferred_element_type=F32)
            acc[i, span] = term if fresh else acc[i, span] + term

    own = pltpu.make_async_copy(piece(me), place(me, mine), own_sem.at[0])
    loop(1, COLS, lambda k: put(k).start())
    own.start()
    own.wait()

    def phase_own(q):
        loop(0, per, lambda j: others(arrived)(column(q, j)))
        to_x(q).start()
        to_y(q).start()
        core(0, q).start()

    def phase_near(q):
        to_x(q).wait_recv()
        core(1, q).start()
        to_y(q).wait_recv()
        relay(q).start()
        core(2, q).start()
        multiply(q, part_x)
        multiply(q, part_y)

    def phase_core(q):
        for i in range(3):
            core(i, q).wait_recv()
            multiply(q, flip(origins[i], 1))

    def swap_core(q, h):
        return send(
            og.at[some(dense * per, q), lanes(2 * h + 1 - bit_c)],
            t1.at[h, some(dense * per, q)],
            c_send.at[q, h],
            c_recv.at[q, h],
            "member",
            other,
        )

    def finish(q):
        relay(q).wait_recv()
        core(3, q).start()
        multiply(q, part_xy)
        core(3, q).wait_recv()
        multiply(q, flip(part_xy, 1))
        n = w.shape[1]
        split = [acc[i, some(rows * per, q)].reshape(per, 2, PAD, n) for i in range(3)]
        pre_gate = split[0][:, 0].reshape(per * PAD, n)
        pre_up = split[1][:, 0].reshape(per * PAD, n)
        d_hidden = split[2][:, 1].reshape(per * PAD, n)
        logistic = jax.nn.sigmoid(pre_gate)
        activated = pre_gate * logistic
        hidden = (activated * pre_up).astype(BF)
        grad_gate = (
            d_hidden * pre_up * logistic * (1.0 + pre_gate * (1.0 - logistic))
        ).astype(BF)
        grad_up = (d_hidden * activated).astype(BF)
        left = [
            jnp.dot(pack[h], v, preferred_element_type=F32).astype(BF)
            for h, v in ((1, grad_gate), (1, grad_up), (0, hidden))
        ]

        def second(k):
            cols = lanes(k)
            total = jnp.dot(left[0], w[0, :, cols], preferred_element_type=F32)
            total += jnp.dot(left[1], w[1, :, cols], preferred_element_type=F32)
            total += jnp.dot(left[2], w[2, :, cols], preferred_element_type=F32)
            og[some(dense * per, q), cols] = total.astype(BF)

        loop(0, SHARDS, second)
        for h in range(4):
            swap_core(q, h).start()

    loop(0, CHUNKS, phase_own)
    for load in loads:
        load.wait()
    loop(0, CHUNKS, lambda q: multiply(q, mine, True))
    loop(0, CHUNKS, phase_near)
    loop(0, CHUNKS, phase_core)
    finish(0)

    def span(q):
        return some(dense * per, q)

    def swap_pair(q, i):
        return send(
            s1.at[route(q, 2 * (1 - bit_y) + i, 2 * i + 1 - bit_x), span(q)],
            t2.at[i, span(q)],
            y_send.at[q, i],
            y_recv.at[q, i],
            "member",
            route(q, along, across),
        )

    def swap_last(q):
        return send(
            s2.at[1 - route(q, bit_x, bit_y), span(q)],
            t3.at[span(q)],
            x_send.at[q],
            x_recv.at[q],
            "member",
            route(q, across, along),
        )

    def spot(source):
        return out.at[some(rows, source // SHARDS), lanes(lax.rem(source, SHARDS))]

    def deliver(q, j):
        c = column(q, j)
        return send(
            home.at[some(rows, per * q + j)], spot(me), h_send.at[c], h_recv.at[me], "member", c
        )

    def deliver_all(q, step):
        loop(0, per, lambda j: others(lambda c: step(deliver(q, j)))(column(q, j)))

    def add_core(q):
        for h in range(4):
            swap_core(q, h).wait_recv()
            total = og[span(q), lanes(2 * h + bit_c)].astype(F32) + t1[h, span(q)].astype(F32)
            s1[h, span(q)] = total.astype(BF)
        for i in range(2):
            swap_pair(q, i).start()

    def add_pair(q):
        for i in range(2):
            swap_pair(q, i).wait_recv()
            kept = s1[route(q, 2 * bit_y + i, 2 * i + bit_x), span(q)]
            s2[i, span(q)] = (kept.astype(F32) + t2[i, span(q)].astype(F32)).astype(BF)
        swap_last(q).start()

    def add_last(q):
        swap_last(q).wait_recv()
        total = s2[route(q, bit_x, bit_y), span(q)].astype(F32) + t3[span(q)].astype(F32)
        wide = jnp.dot(unpack[...], total.astype(BF), preferred_element_type=F32)
        home[some(rows * per, q)] = wide.astype(BF)
        deliver_all(q, lambda copy: copy.start())

    def step(q):
        finish(q)
        add_core(q - 1)

    loop(1, CHUNKS, step)
    add_core(CHUNKS - 1)
    loop(0, CHUNKS, add_pair)
    loop(1, CHUNKS, add_last)
    add_last(0)
    last = pltpu.make_async_copy(home.at[some(rows, mine)], spot(me), own_sem.at[1])
    last.start()

    def drain(q):
        to_x(q).wait_send()
        to_y(q).wait_send()
        relay(q).wait_send()
        for i in range(4):
            core(i, q).wait_send()
            swap_core(q, i).wait_send()
        for i in range(2):
            swap_pair(q, i).wait_send()
        swap_last(q).wait_send()

    def landed(c):
        send(
            home.at[some(rows, 0)], spot(c), h_send.at[0], h_recv.at[c], "member", other
        ).wait_recv()

    loop(1, COLS, lambda k: put(k).wait_send())
    loop(0, CHUNKS, drain)
    loop(0, CHUNKS, lambda q: deliver_all(q, lambda copy: copy.wait_send()))
    loop(0, COLS, others(landed))
    last.wait()


def remote_call(kernel, specs, shape, scratch, ident):
    return pl.pallas_call(
        kernel,
        out_shape=jax.tree.map(lambda dims: jax.ShapeDtypeStruct(dims, BF), shape,
                               is_leaf=lambda v: isinstance(v[0], int)),
        in_specs=specs,
        out_specs=jax.tree.map(lambda dims: VMEM_SPEC, shape,
                               is_leaf=lambda v: isinstance(v[0], int)),
        scratch_shapes=scratch,
        compiler_params=pltpu.CompilerParams(collective_id=ident, has_side_effects=True),
    )


def packing():
    per = COLS // CHUNKS
    pack = np.zeros((2, per * 2 * CAP, per * PAD), np.float32)
    unpack = np.zeros((per * 2 * PAD, per * 2 * CAP), np.float32)
    for c in range(per):
        for h in range(2):
            for r in range(CAP):
                pack[h, (c * 2 + h) * CAP + r, c * PAD + r] = 1
                unpack[(c * 2 + h) * PAD + r, (c * 2 + h) * CAP + r] = 1
    return jnp.asarray(pack, BF), jnp.asarray(unpack, BF)


def body(tokens, cotangent, routes, gate_wts, w_gate, w_up, w_down):
    width = tokens.shape[2]
    dma = pltpu.SemaphoreType.DMA
    pack, unpack = packing()

    experts = lax.axis_index("blk") * EXP_GRP + jnp.arange(EXP_GRP, dtype=jnp.int32)
    match = routes[0][None] == experts[:, None, None]
    named = jnp.sum(match.astype(F32), axis=2)
    weight = jnp.sum(jnp.where(match, gate_wts[0][None], 0.0), axis=2)
    earlier = np.tril(np.ones((COLS, COLS), np.float32), -1)
    rank = jnp.sum(named[:, None, :] * earlier[None], axis=2)
    places = jnp.arange(PAD, dtype=jnp.int32).astype(F32)
    taken = jnp.where(
        (rank[:, None, :] == places[None, :, None]) & (named[:, None, :] > 0), 1.0, 0.0
    )
    both = np.eye(2, dtype=np.float32)[None, :, None, None, :, None]

    def table(values):
        grid = values.reshape(EXP_GRP, 1, PAD, BLKS, 1, COLS // BLKS) * both
        return grid.reshape(EXP_GRP * 2 * PAD, 2 * COLS)

    picker = table(taken).astype(BF)
    combine = table(taken * weight[:, None, :]).T

    pairs = COLS // BLKS
    column = remote_call(
        gather_kernel,
        [VMEM_SPEC] * 2,
        (BLKS, 2, pairs, width),
        [dma((2, 8)), dma((2, 8)), dma((8,)), dma((8,))],
        0,
    )(tokens, cotangent)
    picked = jnp.dot(
        picker, column.reshape(2 * COLS, width), preferred_element_type=F32
    ).astype(BF)
    dense, padded, piece = COLS * 2 * CAP, COLS * 2 * PAD, width // SHARDS
    hidden = w_gate.shape[1]
    sums = remote_call(
        layer_kernel,
        [VMEM_SPEC] + [pl.BlockSpec(memory_space=pl.ANY)] * 3 + [VMEM_SPEC] * 2,
        (EXP_GRP * 2 * PAD, width),
        [
            pltpu.VMEM((padded, width), BF),
            pltpu.VMEM((3, hidden, width), BF),
            pltpu.VMEM((3, padded, hidden), F32),
            pltpu.VMEM((dense, width), BF),
            pltpu.VMEM((4, dense, piece), BF),
            pltpu.VMEM((4, dense, piece), BF),
            pltpu.VMEM((2, dense, piece), BF),
            pltpu.VMEM((2, dense, piece), BF),
            pltpu.VMEM((dense, piece), BF),
            pltpu.VMEM((padded, piece), BF),
            dma((COLS,)),
            dma((COLS,)),
            dma((2,)),
            dma((3,)),
            dma((7, CHUNKS)),
            dma((7, CHUNKS)),
            dma((CHUNKS, 4)),
            dma((CHUNKS, 4)),
            dma((CHUNKS, 2)),
            dma((CHUNKS, 2)),
            dma((CHUNKS,)),
            dma((CHUNKS,)),
            dma((COLS,)),
            dma((COLS,)),
        ],
        1,
    )(picked, w_gate, w_up, w_down, pack, unpack)
    mixed = jnp.dot(
        combine, sums.astype(F32), precision=lax.Precision.HIGHEST, preferred_element_type=F32
    ).astype(BF)
    half = (BLKS // 2, 2, pairs, width)
    return remote_call(
        swap_kernel,
        [VMEM_SPEC],
        ((1, pairs, width), (1, pairs, width)),
        [pltpu.VMEM(half, BF)] * 3 + [dma((8,))] * 4,
        2,
    )(mixed.reshape(BLKS, 2, pairs, width))


def solution(mesh):
    placed = (
        P("member", "blk", None),
        P("member", "blk", None),
        P("member", None, None),
        P("member", None, None),
        P("blk", "member", None),
        P("blk", "member", None),
        P("blk", "member", None),
    )
    return jax.shard_map(
        body,
        mesh=mesh,
        in_specs=placed,
        out_specs=(P("member", "blk", None), P("member", "blk", None)),
        check_vma=False,
    )
```

```python
import jax
import jax.numpy as jnp
import numpy as np
from jax import lax
from jax.experimental import pallas as pl
from jax.experimental.pallas import tpu as pltpu
from jax.sharding import PartitionSpec as P

MESH = pl.DeviceIdType.MESH
EXP_GRP = 4
CAP = 6
PAD = 8
SHARDS = 8
COLS = 32
BLKS = 16
BF = jnp.bfloat16
F32 = jnp.float32
NT = (((1,), (1,)), ((), ()))
VMEM_SPEC = pl.BlockSpec(memory_space=pltpu.VMEM)
CHUNKS = 4


def loop(start, stop, step):
    def run(k, carry):
        step(k)
        return carry

    lax.fori_loop(start, stop, run, 0)


def greet(axis, me, n, meanwhile):
    barrier = pltpu.get_barrier_semaphore()
    loop(
        1,
        n,
        lambda k: pl.semaphore_signal(
            barrier, inc=1, device_id={axis: lax.rem(me + k, n)}, device_id_type=MESH
        ),
    )
    meanwhile()
    pl.semaphore_wait(barrier, n - 1)


def send(src, dst, send_sem, recv_sem, axis, peer):
    return pltpu.make_async_remote_copy(
        src_ref=src,
        dst_ref=dst,
        send_sem=send_sem,
        recv_sem=recv_sem,
        device_id={axis: peer},
        device_id_type=MESH,
    )


def flip(m, w):
    return m + w - 2 * w * lax.rem(m // w, 2)


def greet_few(axis, peers):
    barrier = pltpu.get_barrier_semaphore()
    for peer in peers:
        pl.semaphore_signal(barrier, inc=1, device_id={axis: peer}, device_id_type=MESH)
    pl.semaphore_wait(barrier, len(peers))


FAR_FIRST = (4, 3, 5, 2, 6, 1, 7)
NEAR_FIRST = (1, 7, 2, 6, 3, 5, 4)


def gather_kernel(x, g, out, send_sem, recv_sem, pass_send, pass_recv):
    me = lax.axis_index("blk")
    partner = flip(me, 1)
    ahead = {k: lax.rem(me + 2 * k, BLKS) for k in range(1, 8)}
    greet_few("blk", [ahead[k] for k in FAR_FIRST] + [partner])

    def first(k, peer):
        return [
            send(src.at[0], out.at[me, h], send_sem.at[h, k], recv_sem.at[h, k], "blk", peer)
            for h, src in enumerate((x, g))
        ]

    def passed(k, source):
        return send(
            out.at[source], out.at[source], pass_send.at[k], pass_recv.at[k], "blk", partner
        )

    direct = {k: first(k, ahead[k]) for k in FAR_FIRST}
    direct[0] = first(0, partner)
    for k in FAR_FIRST + (0,):
        for c in direct[k]:
            c.start()
    out[me, 0] = x[0]
    out[me, 1] = g[0]
    relays = []
    for k in NEAR_FIRST:
        for c in direct[k]:
            c.wait_recv()
        relay = passed(k, lax.rem(me + BLKS - 2 * k, BLKS))
        relay.start()
        relays.append(relay)
    for c in direct[0]:
        c.wait_recv()
    for k in FAR_FIRST + (0,):
        for c in direct[k]:
            c.wait_send()
    for relay in relays:
        relay.wait()


def swap_kernel(src, out_a, out_b, near, mid, far, send_sem, recv_sem, far_send, far_recv):
    me = lax.axis_index("blk")
    partner = flip(me, 1)
    ahead = {k: lax.rem(me + 2 * k, BLKS) for k in range(8)}
    greet_few("blk", [ahead[k] for k in FAR_FIRST] + [partner])

    def pair(k):
        return send(
            src.at[flip(ahead[k], 1)],
            near.at[flip(ahead[k], 1) // 2],
            send_sem.at[k],
            recv_sem.at[k],
            "blk",
            partner,
        )

    def along(k):
        return send(mid.at[k], far.at[k], far_send.at[k], far_recv.at[k], "blk", ahead[k])

    order = FAR_FIRST + (0,)
    for k in order:
        pair(k).start()
    for k in order:
        pair(k).wait_recv()
        total = src[ahead[k]].astype(F32) + near[ahead[k] // 2].astype(F32)
        if k:
            mid[k] = total.astype(BF)
            along(k).start()
    for k in NEAR_FIRST:
        along(k).wait_recv()
        total = total + far[k].astype(F32)
    out_a[0] = total[0].astype(BF)
    out_b[0] = total[1].astype(BF)
    for k in order:
        pair(k).wait_send()
        if k:
            along(k).wait_send()


def layer_kernel(
    both_ref, picks, gate, up, down, pack, unpack, out,
    src, rows_ref, w, acc, acc_rest, og, t1, s1, t2, s2, t3, home,
    send_sem, recv_sem, own_sem, w_sem, hop_send, hop_recv,
    c_send, c_recv, y_send, y_recv, x_send, x_recv, h_send, h_recv,
):
    me = lax.axis_index("member")
    width = both_ref.shape[1] // SHARDS
    lane = width // 4
    thin = width - lane
    n = w.shape[0] // 3
    rows = 2 * PAD
    dense = 2 * CAP
    per = COLS // CHUNKS
    mine = lax.rem(me, SHARDS)
    bit_c, bit_x, bit_y = lax.rem(me, 2), lax.rem(me // 2, 2), lax.rem(me // 4, 2)
    across, along, other = flip(me, 2), flip(me, 4), flip(me, 1)
    part_x, part_y = flip(mine, 2), flip(mine, 4)
    part_xy = flip(part_x, 4)

    loads = [
        pltpu.make_async_copy(ref.at[0], w.at[pl.ds(n * i, n)], w_sem.at[i])
        for i, ref in enumerate((gate, up, down))
    ]
    for load in loads:
        load.start()
    def some(size, at):
        return pl.ds(pl.multiple_of(size * at, size), size)

    def lanes(part):
        return some(width, part)

    def pick(j):
        sums = jnp.dot(picks[...], both_ref[:, lanes(j)], preferred_element_type=F32)
        tall = src.shape[0]
        for t in range(3):
            tile = sums[:tall, lane * t : lane * (t + 1)]
            tile = tile + sums[tall * (t + 1) : tall * (t + 2), thin:]
            src[:, some(lane, 3 * j + t)] = tile.astype(BF)

    greet("member", me, COLS, lambda: loop(0, SHARDS, pick))

    def piece(peer):
        return src.at[some(rows, peer // SHARDS), some(thin, lax.rem(peer, SHARDS))]

    def place(col, part):
        return rows_ref.at[some(rows, col), some(thin, part)]

    slot = me // SHARDS

    def chunk(q):
        return lax.rem(slot + q + (q // 2) * (1 - 2 * (q % 2)), CHUNKS)

    def column(q, j):
        return per * chunk(q) + j

    def put(k):
        peer = column(k // per, lax.rem(mine + k, per))
        return send(
            piece(peer),
            place(me, lax.rem(peer, SHARDS)),
            send_sem.at[k],
            recv_sem.at[me],
            "member",
            peer,
        )

    def others(step):
        def run(c):
            @pl.when(c != me)
            def _():
                step(c)

        return run

    def arrived(c):
        send(
            place(c, mine), place(c, mine), send_sem.at[0], recv_sem.at[c], "member", other
        ).wait_recv()

    def hop(kind, q, origin, peer):
        part = rows_ref.at[some(rows * per, chunk(q)), some(thin, origin)]
        return send(part, part, hop_send.at[kind, q], hop_recv.at[kind, q], "member", peer)

    to_x = lambda q: hop(0, q, mine, across)
    to_y = lambda q: hop(1, q, mine, along)

    def route(q, relay_y, relay_x):
        late = (q + CHUNKS - 1) // CHUNKS
        return (1 - late) * relay_y + late * relay_x

    relay = lambda q: hop(2, q, route(q, part_x, part_y), route(q, along, across))
    origins = (mine, part_x, part_y, part_xy)
    core = lambda i, q: hop(3 + i, q, origins[i], other)

    def multiply(q, origin, fresh=False):
        span = some(rows * per, q)
        left = rows_ref[some(rows * per, chunk(q)), some(thin, origin)]
        near = w[:, pl.ds(pl.multiple_of(width * origin, width), thin)]
        rest = w[:, pl.ds(pl.multiple_of(width * origin + thin, lane), lane)]
        term = lax.dot_general(left, near, NT, preferred_element_type=F32)
        acc[span] = term if fresh else acc[span] + term
        tiles = jnp.concatenate([left[:, lane * t : lane * (t + 1)] for t in range(3)], axis=0)
        term = lax.dot_general(tiles, rest, NT, preferred_element_type=F32)
        for t in range(3):
            part = term[rows * per * t : rows * per * (t + 1)]
            acc_rest[t, span] = part if fresh else acc_rest[t, span] + part

    own = pltpu.make_async_copy(piece(me), place(me, mine), own_sem.at[0])
    loop(1, COLS, lambda k: put(k).start())
    own.start()
    own.wait()

    def phase_own(q):
        loop(0, per, lambda j: others(arrived)(column(q, j)))
        to_x(q).start()
        to_y(q).start()
        core(0, q).start()

    def phase_near(q):
        to_x(q).wait_recv()
        core(1, q).start()
        to_y(q).wait_recv()
        relay(q).start()
        core(2, q).start()
        multiply(q, part_x)
        multiply(q, part_y)

    def phase_core(q):
        for i in range(3):
            core(i, q).wait_recv()
            multiply(q, flip(origins[i], 1))

    def swap_core(q, h):
        return send(
            og.at[some(dense * per, q), lanes(2 * h + 1 - bit_c)],
            t1.at[h, some(dense * per, q)],
            c_send.at[q, h],
            c_recv.at[q, h],
            "member",
            other,
        )

    def finish(q):
        relay(q).wait_recv()
        core(3, q).start()
        multiply(q, part_xy)
        core(3, q).wait_recv()
        multiply(q, flip(part_xy, 1))
        at = lax.broadcasted_iota(jnp.int32, (per, PAD, n), 1)

        def whole(i, h):
            cols = slice(n * i, n * (i + 1))
            value = acc[some(rows * per, q), cols].reshape(per, 2, PAD, n)[:, h]
            for t in range(3):
                rest = acc_rest[t, some(rows * per, q), cols].reshape(per, 2, PAD, n)[:, h]
                here = (at >= 2 * t) & (at < 2 * t + 2)
                value = value + jnp.where(here, pltpu.roll(rest, 2 * t + 2, 1), 0.0)
            return value.reshape(per * PAD, n)

        pre_gate, pre_up, d_hidden = whole(0, 0), whole(1, 0), whole(2, 1)
        logistic = jax.nn.sigmoid(pre_gate)
        activated = pre_gate * logistic
        hidden = (activated * pre_up).astype(BF)
        grad_gate = (
            d_hidden * pre_up * logistic * (1.0 + pre_gate * (1.0 - logistic))
        ).astype(BF)
        grad_up = (d_hidden * activated).astype(BF)
        left = [
            jnp.dot(pack[h], v, preferred_element_type=F32).astype(BF)
            for h, v in ((1, grad_gate), (1, grad_up), (0, hidden))
        ]
        left = jnp.concatenate(left, axis=1)

        def second(k):
            cols = lanes(k)
            total = jnp.dot(left, w[:, cols], preferred_element_type=F32)
            og[some(dense * per, q), cols] = total.astype(BF)

        loop(0, SHARDS, second)
        for h in range(4):
            swap_core(q, h).start()

    loop(0, CHUNKS, phase_own)
    for load in loads:
        load.wait()
    loop(0, CHUNKS, lambda q: multiply(q, mine, True))
    loop(0, CHUNKS, phase_near)
    loop(0, CHUNKS, phase_core)
    finish(0)

    def span(q):
        return some(dense * per, q)

    def swap_pair(q, i):
        return send(
            s1.at[route(q, 2 * (1 - bit_y) + i, 2 * i + 1 - bit_x), span(q)],
            t2.at[i, span(q)],
            y_send.at[q, i],
            y_recv.at[q, i],
            "member",
            route(q, along, across),
        )

    def swap_last(q):
        return send(
            s2.at[1 - route(q, bit_x, bit_y), span(q)],
            t3.at[span(q)],
            x_send.at[q],
            x_recv.at[q],
            "member",
            route(q, across, along),
        )

    def spot(source):
        return out.at[some(rows, source // SHARDS), lanes(lax.rem(source, SHARDS))]

    def deliver(q, j):
        c = column(q, j)
        return send(
            home.at[some(rows, per * q + j)], spot(me), h_send.at[c], h_recv.at[me], "member", c
        )

    def deliver_all(q, step):
        loop(0, per, lambda j: others(lambda c: step(deliver(q, j)))(column(q, j)))

    def add_core(q):
        for h in range(4):
            swap_core(q, h).wait_recv()
            total = og[span(q), lanes(2 * h + bit_c)].astype(F32) + t1[h, span(q)].astype(F32)
            s1[h, span(q)] = total.astype(BF)
        for i in range(2):
            swap_pair(q, i).start()

    def add_pair(q):
        for i in range(2):
            swap_pair(q, i).wait_recv()
            kept = s1[route(q, 2 * bit_y + i, 2 * i + bit_x), span(q)]
            s2[i, span(q)] = (kept.astype(F32) + t2[i, span(q)].astype(F32)).astype(BF)
        swap_last(q).start()

    def add_last(q):
        swap_last(q).wait_recv()
        total = s2[route(q, bit_x, bit_y), span(q)].astype(F32) + t3[span(q)].astype(F32)
        wide = jnp.dot(unpack[...], total.astype(BF), preferred_element_type=F32)
        home[some(rows * per, q)] = wide.astype(BF)
        deliver_all(q, lambda copy: copy.start())

    def step(q):
        finish(q)
        add_core(q - 1)

    loop(1, CHUNKS, step)
    add_core(CHUNKS - 1)
    loop(0, CHUNKS, add_pair)
    loop(1, CHUNKS, add_last)
    add_last(0)
    last = pltpu.make_async_copy(home.at[some(rows, mine)], spot(me), own_sem.at[1])
    last.start()

    def drain(q):
        to_x(q).wait_send()
        to_y(q).wait_send()
        relay(q).wait_send()
        for i in range(4):
            core(i, q).wait_send()
            swap_core(q, i).wait_send()
        for i in range(2):
            swap_pair(q, i).wait_send()
        swap_last(q).wait_send()

    def landed(c):
        send(
            home.at[some(rows, 0)], spot(c), h_send.at[0], h_recv.at[c], "member", other
        ).wait_recv()

    loop(1, COLS, lambda k: put(k).wait_send())
    loop(0, CHUNKS, drain)
    loop(0, CHUNKS, lambda q: deliver_all(q, lambda copy: copy.wait_send()))
    loop(0, COLS, others(landed))
    last.wait()


def remote_call(kernel, specs, shape, scratch, ident):
    return pl.pallas_call(
        kernel,
        out_shape=jax.tree.map(lambda dims: jax.ShapeDtypeStruct(dims, BF), shape,
                               is_leaf=lambda v: isinstance(v[0], int)),
        in_specs=specs,
        out_specs=jax.tree.map(lambda dims: VMEM_SPEC, shape,
                               is_leaf=lambda v: isinstance(v[0], int)),
        scratch_shapes=scratch,
        compiler_params=pltpu.CompilerParams(collective_id=ident, has_side_effects=True),
    )


def packing():
    per = COLS // CHUNKS
    pack = np.zeros((2, per * 2 * CAP, per * PAD), np.float32)
    unpack = np.zeros((per * 2 * PAD, per * 2 * CAP), np.float32)
    for c in range(per):
        for h in range(2):
            for r in range(CAP):
                pack[h, (c * 2 + h) * CAP + r, c * PAD + r] = 1
                unpack[(c * 2 + h) * PAD + r, (c * 2 + h) * CAP + r] = 1
    spread = np.zeros((4, EXP_GRP * 2, PAD, EXP_GRP * 2, PAD), np.float32)
    for e in range(EXP_GRP * 2):
        for r in range(CAP):
            spread[0, e, r, e, r] = 1
            spread[1 + r // 2, e, CAP + r % 2, e, r] = 1
    spread = spread.reshape(4 * EXP_GRP * 2 * PAD, EXP_GRP * 2 * PAD)
    return jnp.asarray(pack, BF), jnp.asarray(unpack, BF), jnp.asarray(spread, BF)


def body(tokens, cotangent, routes, gate_wts, w_gate, w_up, w_down):
    width = tokens.shape[2]
    dma = pltpu.SemaphoreType.DMA
    pack, unpack, spread = packing()

    experts = lax.axis_index("blk") * EXP_GRP + jnp.arange(EXP_GRP, dtype=jnp.int32)
    match = routes[0][None] == experts[:, None, None]
    named = jnp.sum(match.astype(F32), axis=2)
    weight = jnp.sum(jnp.where(match, gate_wts[0][None], 0.0), axis=2)
    earlier = np.tril(np.ones((COLS, COLS), np.float32), -1)
    rank = jnp.sum(named[:, None, :] * earlier[None], axis=2)
    places = jnp.arange(PAD, dtype=jnp.int32).astype(F32)
    taken = jnp.where(
        (rank[:, None, :] == places[None, :, None]) & (named[:, None, :] > 0), 1.0, 0.0
    )
    both = np.eye(2, dtype=np.float32)[None, :, None, None, :, None]

    def table(values):
        grid = values.reshape(EXP_GRP, 1, PAD, BLKS, 1, COLS // BLKS) * both
        return grid.reshape(EXP_GRP * 2 * PAD, 2 * COLS)

    picks = jnp.dot(spread, table(taken).astype(BF), preferred_element_type=F32).astype(BF)
    combine = table(taken * weight[:, None, :]).T

    pairs = COLS // BLKS
    column = remote_call(
        gather_kernel,
        [VMEM_SPEC] * 2,
        (BLKS, 2, pairs, width),
        [dma((2, 8)), dma((2, 8)), dma((8,)), dma((8,))],
        0,
    )(tokens, cotangent)
    dense, padded, piece = COLS * 2 * CAP, COLS * 2 * PAD, width // SHARDS
    hidden = w_gate.shape[1]
    sums = remote_call(
        layer_kernel,
        [VMEM_SPEC] * 2 + [pl.BlockSpec(memory_space=pl.ANY)] * 3 + [VMEM_SPEC] * 2,
        (EXP_GRP * 2 * PAD, width),
        [
            pltpu.VMEM((EXP_GRP * 2 * PAD, width // 4 * 3), BF),
            pltpu.VMEM((padded, width // 4 * 3), BF),
            pltpu.VMEM((3 * hidden, width), BF),
            pltpu.VMEM((padded, 3 * hidden), F32),
            pltpu.VMEM((3, padded, 3 * hidden), F32),
            pltpu.VMEM((dense, width), BF),
            pltpu.VMEM((4, dense, piece), BF),
            pltpu.VMEM((4, dense, piece), BF),
            pltpu.VMEM((2, dense, piece), BF),
            pltpu.VMEM((2, dense, piece), BF),
            pltpu.VMEM((dense, piece), BF),
            pltpu.VMEM((padded, piece), BF),
            dma((COLS,)),
            dma((COLS,)),
            dma((2,)),
            dma((3,)),
            dma((7, CHUNKS)),
            dma((7, CHUNKS)),
            dma((CHUNKS, 4)),
            dma((CHUNKS, 4)),
            dma((CHUNKS, 2)),
            dma((CHUNKS, 2)),
            dma((CHUNKS,)),
            dma((CHUNKS,)),
            dma((COLS,)),
            dma((COLS,)),
        ],
        1,
    )(column.reshape(2 * COLS, width), picks, w_gate, w_up, w_down, pack, unpack)
    mixed = jnp.dot(
        combine, sums.astype(F32), precision=lax.Precision.HIGHEST, preferred_element_type=F32
    ).astype(BF)
    half = (BLKS // 2, 2, pairs, width)
    return remote_call(
        swap_kernel,
        [VMEM_SPEC],
        ((1, pairs, width), (1, pairs, width)),
        [pltpu.VMEM(half, BF)] * 3 + [dma((8,))] * 4,
        2,
    )(mixed.reshape(BLKS, 2, pairs, width))


def solution(mesh):
    placed = (
        P("member", "blk", None),
        P("member", "blk", None),
        P("member", None, None),
        P("member", None, None),
        P("blk", "member", None),
        P("blk", "member", None),
        P("blk", "member", None),
    )
    return jax.shard_map(
        body,
        mesh=mesh,
        in_specs=placed,
        out_specs=(P("member", "blk", None), P("member", "blk", None)),
        check_vma=False,
    )
```

```python
import jax
import jax.numpy as jnp
import numpy as np
from jax import lax
from jax.experimental import pallas as pl
from jax.experimental.pallas import tpu as pltpu
from jax.sharding import PartitionSpec as P

MESH = pl.DeviceIdType.MESH
EXP_GRP = 4
CAP = 6
PAD = 8
SHARDS = 8
COLS = 32
BLKS = 16
BF = jnp.bfloat16
F32 = jnp.float32
NT = (((1,), (1,)), ((), ()))
VMEM_SPEC = pl.BlockSpec(memory_space=pltpu.VMEM)
CHUNKS = 4


def loop(start, stop, step):
    def run(k, carry):
        step(k)
        return carry

    lax.fori_loop(start, stop, run, 0)


def greet(axis, me, n, meanwhile):
    barrier = pltpu.get_barrier_semaphore()
    loop(
        1,
        n,
        lambda k: pl.semaphore_signal(
            barrier, inc=1, device_id={axis: lax.rem(me + k, n)}, device_id_type=MESH
        ),
    )
    meanwhile()
    pl.semaphore_wait(barrier, n - 1)


def send(src, dst, send_sem, recv_sem, axis, peer):
    return pltpu.make_async_remote_copy(
        src_ref=src,
        dst_ref=dst,
        send_sem=send_sem,
        recv_sem=recv_sem,
        device_id={axis: peer},
        device_id_type=MESH,
    )


def row_pairs():
    pairs = COLS // BLKS
    for i in range(2 * BLKS):
        yield i // 2, i % 2, slice(pairs * i, pairs * (i + 1))


def flip(m, w):
    return m + w - 2 * w * lax.rem(m // w, 2)


def greet_few(axis, peers, meanwhile=lambda: None):
    barrier = pltpu.get_barrier_semaphore()
    for peer in peers:
        pl.semaphore_signal(barrier, inc=1, device_id={axis: peer}, device_id_type=MESH)
    meanwhile()
    pl.semaphore_wait(barrier, len(peers))


FAR_FIRST = (4, 3, 5, 2, 6, 1, 7)
NEAR_FIRST = (1, 7, 2, 6, 3, 5, 4)


def gather_kernel(x, g, out, send_sem, recv_sem, pass_send, pass_recv):
    me = lax.axis_index("blk")
    partner = flip(me, 1)
    ahead = {k: lax.rem(me + 2 * k, BLKS) for k in range(1, 8)}
    greet_few("blk", [ahead[k] for k in FAR_FIRST] + [partner])

    def first(k, peer):
        return [
            send(src.at[0], out.at[me, h], send_sem.at[h, k], recv_sem.at[h, k], "blk", peer)
            for h, src in enumerate((x, g))
        ]

    def passed(k, source):
        return send(
            out.at[source], out.at[source], pass_send.at[k], pass_recv.at[k], "blk", partner
        )

    direct = {k: first(k, ahead[k]) for k in FAR_FIRST}
    direct[0] = first(0, partner)
    for k in FAR_FIRST + (0,):
        for c in direct[k]:
            c.start()
    out[me, 0] = x[0]
    out[me, 1] = g[0]
    relays = []
    for k in NEAR_FIRST:
        for c in direct[k]:
            c.wait_recv()
        relay = passed(k, lax.rem(me + BLKS - 2 * k, BLKS))
        relay.start()
        relays.append(relay)
    for c in direct[0]:
        c.wait_recv()
    for k in FAR_FIRST + (0,):
        for c in direct[k]:
            c.wait_send()
    for relay in relays:
        relay.wait()


def swap_kernel(
    sums, combine, out_a, out_b, mixed, src, near, mid, far, send_sem, recv_sem, far_send, far_recv
):
    me = lax.axis_index("blk")
    partner = flip(me, 1)
    ahead = {k: lax.rem(me + 2 * k, BLKS) for k in range(8)}
    width = sums.shape[1] // SHARDS

    def mix(j):
        cols = pl.ds(pl.multiple_of(width * j, width), width)
        mixed[:, cols] = jnp.dot(
            combine[...],
            sums[:, cols].astype(F32),
            precision=lax.Precision.HIGHEST,
            preferred_element_type=F32,
        )

    def prepare():
        loop(0, SHARDS, mix)
        for p, h, at in row_pairs():
            src[p, h] = mixed[at].astype(BF)

    greet_few("blk", [ahead[k] for k in FAR_FIRST] + [partner], prepare)

    def pair(k):
        return send(
            src.at[flip(ahead[k], 1)],
            near.at[flip(ahead[k], 1) // 2],
            send_sem.at[k],
            recv_sem.at[k],
            "blk",
            partner,
        )

    def along(k):
        return send(mid.at[k], far.at[k], far_send.at[k], far_recv.at[k], "blk", ahead[k])

    order = FAR_FIRST + (0,)
    for k in order:
        pair(k).start()
    for k in order:
        pair(k).wait_recv()
        total = src[ahead[k]].astype(F32) + near[ahead[k] // 2].astype(F32)
        if k:
            mid[k] = total.astype(BF)
            along(k).start()
    for k in NEAR_FIRST:
        along(k).wait_recv()
        total = total + far[k].astype(F32)
    out_a[0] = total[0].astype(BF)
    out_b[0] = total[1].astype(BF)
    for k in order:
        pair(k).wait_send()
        if k:
            along(k).wait_send()


def layer_kernel(
    both_ref, picks, gate, up, down, pack, unpack, out,
    flat, src, rows_ref, w, acc, acc_rest, og, t1, s1, t2, s2, t3, home,
    send_sem, recv_sem, own_sem, w_sem, hop_send, hop_recv,
    c_send, c_recv, y_send, y_recv, x_send, x_recv, h_send, h_recv,
):
    me = lax.axis_index("member")
    width = flat.shape[1] // SHARDS
    lane = width // 4
    thin = width - lane
    n = w.shape[0] // 3
    rows = 2 * PAD
    dense = 2 * CAP
    per = COLS // CHUNKS
    mine = lax.rem(me, SHARDS)
    bit_c, bit_x, bit_y = lax.rem(me, 2), lax.rem(me // 2, 2), lax.rem(me // 4, 2)
    across, along, other = flip(me, 2), flip(me, 4), flip(me, 1)
    part_x, part_y = flip(mine, 2), flip(mine, 4)
    part_xy = flip(part_x, 4)

    loads = [
        pltpu.make_async_copy(ref.at[0], w.at[pl.ds(n * i, n)], w_sem.at[i])
        for i, ref in enumerate((gate, up, down))
    ]
    for load in loads:
        load.start()
    def some(size, at):
        return pl.ds(pl.multiple_of(size * at, size), size)

    def lanes(part):
        return some(width, part)

    def pick(j):
        sums = jnp.dot(picks[...], flat[:, lanes(j)].astype(BF), preferred_element_type=F32)
        tall = src.shape[0]
        for t in range(3):
            tile = sums[:tall, lane * t : lane * (t + 1)]
            tile = tile + sums[tall * (t + 1) : tall * (t + 2), thin:]
            src[:, some(lane, 3 * j + t)] = tile.astype(BF)

    def regroup():
        for p, h, at in row_pairs():
            flat[at] = both_ref[p, h].astype(F32)
        loop(0, SHARDS, pick)

    greet("member", me, COLS, regroup)

    def piece(peer):
        return src.at[some(rows, peer // SHARDS), some(thin, lax.rem(peer, SHARDS))]

    def place(col, part):
        return rows_ref.at[some(rows, col), some(thin, part)]

    slot = me // SHARDS

    def chunk(q):
        return lax.rem(slot + q + (q // 2) * (1 - 2 * (q % 2)), CHUNKS)

    def column(q, j):
        return per * chunk(q) + j

    def put(k):
        peer = column(k // per, lax.rem(mine + k, per))
        return send(
            piece(peer),
            place(me, lax.rem(peer, SHARDS)),
            send_sem.at[k],
            recv_sem.at[me],
            "member",
            peer,
        )

    def others(step):
        def run(c):
            @pl.when(c != me)
            def _():
                step(c)

        return run

    def arrived(c):
        send(
            place(c, mine), place(c, mine), send_sem.at[0], recv_sem.at[c], "member", other
        ).wait_recv()

    def hop(kind, q, origin, peer):
        part = rows_ref.at[some(rows * per, chunk(q)), some(thin, origin)]
        return send(part, part, hop_send.at[kind, q], hop_recv.at[kind, q], "member", peer)

    to_x = lambda q: hop(0, q, mine, across)
    to_y = lambda q: hop(1, q, mine, along)

    def route(q, relay_y, relay_x):
        late = (q + CHUNKS - 1) // CHUNKS
        return (1 - late) * relay_y + late * relay_x

    relay = lambda q: hop(2, q, route(q, part_x, part_y), route(q, along, across))
    origins = (mine, part_x, part_y, part_xy)
    core = lambda i, q: hop(3 + i, q, origins[i], other)

    def multiply(q, origin, fresh=False):
        span = some(rows * per, q)
        left = rows_ref[some(rows * per, chunk(q)), some(thin, origin)]
        near = w[:, pl.ds(pl.multiple_of(width * origin, width), thin)]
        rest = w[:, pl.ds(pl.multiple_of(width * origin + thin, lane), lane)]
        term = lax.dot_general(left, near, NT, preferred_element_type=F32)
        acc[span] = term if fresh else acc[span] + term
        tiles = jnp.concatenate([left[:, lane * t : lane * (t + 1)] for t in range(3)], axis=0)
        term = lax.dot_general(tiles, rest, NT, preferred_element_type=F32)
        for t in range(3):
            part = term[rows * per * t : rows * per * (t + 1)]
            acc_rest[t, span] = part if fresh else acc_rest[t, span] + part

    own = pltpu.make_async_copy(piece(me), place(me, mine), own_sem.at[0])
    loop(1, COLS, lambda k: put(k).start())
    own.start()
    own.wait()

    def phase_own(q):
        loop(0, per, lambda j: others(arrived)(column(q, j)))
        to_x(q).start()
        to_y(q).start()
        core(0, q).start()

    def phase_near(q):
        to_x(q).wait_recv()
        core(1, q).start()
        to_y(q).wait_recv()
        relay(q).start()
        core(2, q).start()
        multiply(q, part_x)
        multiply(q, part_y)

    def phase_core(q):
        for i in range(3):
            core(i, q).wait_recv()
            multiply(q, flip(origins[i], 1))

    def swap_core(q, h):
        return send(
            og.at[some(dense * per, q), lanes(2 * h + 1 - bit_c)],
            t1.at[h, some(dense * per, q)],
            c_send.at[q, h],
            c_recv.at[q, h],
            "member",
            other,
        )

    def near_done(q):
        relay(q).wait_recv()
        core(3, q).start()
        multiply(q, part_xy)

    def finish(q):
        core(3, q).wait_recv()
        multiply(q, flip(part_xy, 1))
        at = lax.broadcasted_iota(jnp.int32, (per, PAD, n), 1)

        def whole(i, h):
            cols = slice(n * i, n * (i + 1))
            value = acc[some(rows * per, q), cols].reshape(per, 2, PAD, n)[:, h]
            for t in range(3):
                rest = acc_rest[t, some(rows * per, q), cols].reshape(per, 2, PAD, n)[:, h]
                here = (at >= 2 * t) & (at < 2 * t + 2)
                value = value + jnp.where(here, pltpu.roll(rest, 2 * t + 2, 1), 0.0)
            return value.reshape(per * PAD, n)

        pre_gate, pre_up, d_hidden = whole(0, 0), whole(1, 0), whole(2, 1)
        logistic = jax.nn.sigmoid(pre_gate)
        activated = pre_gate * logistic
        hidden = (activated * pre_up).astype(BF)
        grad_gate = (
            d_hidden * pre_up * logistic * (1.0 + pre_gate * (1.0 - logistic))
        ).astype(BF)
        grad_up = (d_hidden * activated).astype(BF)
        left = [
            jnp.dot(pack[h], v, preferred_element_type=F32).astype(BF)
            for h, v in ((1, grad_gate), (1, grad_up), (0, hidden))
        ]
        left = jnp.concatenate(left, axis=1)

        def second(k):
            cols = lanes(k)
            total = jnp.dot(left, w[:, cols], preferred_element_type=F32)
            og[some(dense * per, q), cols] = total.astype(BF)

        loop(0, SHARDS, second)
        for h in range(4):
            swap_core(q, h).start()

    loop(0, CHUNKS, phase_own)
    for load in loads:
        load.wait()
    loop(0, CHUNKS, lambda q: multiply(q, mine, True))
    loop(0, CHUNKS, phase_near)
    loop(0, CHUNKS, phase_core)
    near_done(0)
    near_done(1)
    finish(0)

    def span(q):
        return some(dense * per, q)

    def swap_pair(q, i):
        return send(
            s1.at[route(q, 2 * (1 - bit_y) + i, 2 * i + 1 - bit_x), span(q)],
            t2.at[i, span(q)],
            y_send.at[q, i],
            y_recv.at[q, i],
            "member",
            route(q, along, across),
        )

    def swap_last(q):
        return send(
            s2.at[1 - route(q, bit_x, bit_y), span(q)],
            t3.at[span(q)],
            x_send.at[q],
            x_recv.at[q],
            "member",
            route(q, across, along),
        )

    def spot(source):
        return out.at[some(rows, source // SHARDS), lanes(lax.rem(source, SHARDS))]

    def deliver(q, j):
        c = column(q, j)
        return send(
            home.at[some(rows, per * q + j)], spot(me), h_send.at[c], h_recv.at[me], "member", c
        )

    def deliver_all(q, step):
        loop(0, per, lambda j: others(lambda c: step(deliver(q, j)))(column(q, j)))

    def add_core(q):
        for h in range(4):
            swap_core(q, h).wait_recv()
            total = og[span(q), lanes(2 * h + bit_c)].astype(F32) + t1[h, span(q)].astype(F32)
            s1[h, span(q)] = total.astype(BF)
        for i in range(2):
            swap_pair(q, i).start()

    def add_pair(q):
        for i in range(2):
            swap_pair(q, i).wait_recv()
            kept = s1[route(q, 2 * bit_y + i, 2 * i + bit_x), span(q)]
            s2[i, span(q)] = (kept.astype(F32) + t2[i, span(q)].astype(F32)).astype(BF)
        swap_last(q).start()

    def add_last(q):
        swap_last(q).wait_recv()
        total = s2[route(q, bit_x, bit_y), span(q)].astype(F32) + t3[span(q)].astype(F32)
        wide = jnp.dot(unpack[...], total.astype(BF), preferred_element_type=F32)
        home[some(rows * per, q)] = wide.astype(BF)
        deliver_all(q, lambda copy: copy.start())

    def step(q):
        near_done(q)
        finish(q - 1)
        add_core(q - 2)

    loop(2, CHUNKS, step)
    finish(CHUNKS - 1)
    add_core(CHUNKS - 2)
    add_core(CHUNKS - 1)
    loop(0, CHUNKS, add_pair)
    loop(1, CHUNKS, add_last)
    add_last(0)
    last = pltpu.make_async_copy(home.at[some(rows, mine)], spot(me), own_sem.at[1])
    last.start()

    def drain(q):
        to_x(q).wait_send()
        to_y(q).wait_send()
        relay(q).wait_send()
        for i in range(4):
            core(i, q).wait_send()
            swap_core(q, i).wait_send()
        for i in range(2):
            swap_pair(q, i).wait_send()
        swap_last(q).wait_send()

    def landed(c):
        send(
            home.at[some(rows, 0)], spot(c), h_send.at[0], h_recv.at[c], "member", other
        ).wait_recv()

    loop(1, COLS, lambda k: put(k).wait_send())
    loop(0, CHUNKS, drain)
    loop(0, CHUNKS, lambda q: deliver_all(q, lambda copy: copy.wait_send()))
    loop(0, COLS, others(landed))
    last.wait()


def remote_call(kernel, specs, shape, scratch, ident):
    return pl.pallas_call(
        kernel,
        out_shape=jax.tree.map(lambda dims: jax.ShapeDtypeStruct(dims, BF), shape,
                               is_leaf=lambda v: isinstance(v[0], int)),
        in_specs=specs,
        out_specs=jax.tree.map(lambda dims: VMEM_SPEC, shape,
                               is_leaf=lambda v: isinstance(v[0], int)),
        scratch_shapes=scratch,
        compiler_params=pltpu.CompilerParams(collective_id=ident, has_side_effects=True),
    )


def packing():
    per = COLS // CHUNKS
    pack = np.zeros((2, per * 2 * CAP, per * PAD), np.float32)
    unpack = np.zeros((per * 2 * PAD, per * 2 * CAP), np.float32)
    for c in range(per):
        for h in range(2):
            for r in range(CAP):
                pack[h, (c * 2 + h) * CAP + r, c * PAD + r] = 1
                unpack[(c * 2 + h) * PAD + r, (c * 2 + h) * CAP + r] = 1
    spread = np.zeros((4, EXP_GRP * 2, PAD, EXP_GRP * 2, PAD), np.float32)
    for e in range(EXP_GRP * 2):
        for r in range(CAP):
            spread[0, e, r, e, r] = 1
            spread[1 + r // 2, e, CAP + r % 2, e, r] = 1
    spread = spread.reshape(4 * EXP_GRP * 2 * PAD, EXP_GRP * 2 * PAD)
    return jnp.asarray(pack, BF), jnp.asarray(unpack, BF), jnp.asarray(spread, BF)


def body(tokens, cotangent, routes, gate_wts, w_gate, w_up, w_down):
    width = tokens.shape[2]
    dma = pltpu.SemaphoreType.DMA
    pack, unpack, spread = packing()

    experts = lax.axis_index("blk") * EXP_GRP + jnp.arange(EXP_GRP, dtype=jnp.int32)
    match = routes[0][None] == experts[:, None, None]
    named = jnp.sum(match.astype(F32), axis=2)
    weight = jnp.sum(jnp.where(match, gate_wts[0][None], 0.0), axis=2)
    earlier = np.tril(np.ones((COLS, COLS), np.float32), -1)
    rank = jnp.sum(named[:, None, :] * earlier[None], axis=2)
    places = jnp.arange(PAD, dtype=jnp.int32).astype(F32)
    taken = jnp.where(
        (rank[:, None, :] == places[None, :, None]) & (named[:, None, :] > 0), 1.0, 0.0
    )
    both = np.eye(2, dtype=np.float32)[None, :, None, None, :, None]

    def table(values):
        grid = values.reshape(EXP_GRP, 1, PAD, BLKS, 1, COLS // BLKS) * both
        return grid.reshape(EXP_GRP * 2 * PAD, 2 * COLS)

    picks = jnp.dot(spread, table(taken).astype(BF), preferred_element_type=F32).astype(BF)
    combine = table(taken * weight[:, None, :]).T

    pairs = COLS // BLKS
    column = remote_call(
        gather_kernel,
        [VMEM_SPEC] * 2,
        (BLKS, 2, pairs, width),
        [dma((2, 8)), dma((2, 8)), dma((8,)), dma((8,))],
        0,
    )(tokens, cotangent)
    dense, padded, piece = COLS * 2 * CAP, COLS * 2 * PAD, width // SHARDS
    hidden = w_gate.shape[1]
    sums = remote_call(
        layer_kernel,
        [VMEM_SPEC] * 2 + [pl.BlockSpec(memory_space=pl.ANY)] * 3 + [VMEM_SPEC] * 2,
        (EXP_GRP * 2 * PAD, width),
        [
            pltpu.VMEM((2 * COLS, width), F32),
            pltpu.VMEM((EXP_GRP * 2 * PAD, width // 4 * 3), BF),
            pltpu.VMEM((padded, width // 4 * 3), BF),
            pltpu.VMEM((3 * hidden, width), BF),
            pltpu.VMEM((padded, 3 * hidden), F32),
            pltpu.VMEM((3, padded, 3 * hidden), F32),
            pltpu.VMEM((dense, width), BF),
            pltpu.VMEM((4, dense, piece), BF),
            pltpu.VMEM((4, dense, piece), BF),
            pltpu.VMEM((2, dense, piece), BF),
            pltpu.VMEM((2, dense, piece), BF),
            pltpu.VMEM((dense, piece), BF),
            pltpu.VMEM((padded, piece), BF),
            dma((COLS,)),
            dma((COLS,)),
            dma((2,)),
            dma((3,)),
            dma((7, CHUNKS)),
            dma((7, CHUNKS)),
            dma((CHUNKS, 4)),
            dma((CHUNKS, 4)),
            dma((CHUNKS, 2)),
            dma((CHUNKS, 2)),
            dma((CHUNKS,)),
            dma((CHUNKS,)),
            dma((COLS,)),
            dma((COLS,)),
        ],
        1,
    )(column, picks, w_gate, w_up, w_down, pack, unpack)
    half = (BLKS // 2, 2, pairs, width)
    return remote_call(
        swap_kernel,
        [VMEM_SPEC] * 2,
        ((1, pairs, width), (1, pairs, width)),
        [pltpu.VMEM((2 * COLS, width), F32), pltpu.VMEM((BLKS, 2, pairs, width), BF)]
        + [pltpu.VMEM(half, BF)] * 3
        + [dma((8,))] * 4,
        2,
    )(sums, combine)


def solution(mesh):
    placed = (
        P("member", "blk", None),
        P("member", "blk", None),
        P("member", None, None),
        P("member", None, None),
        P("blk", "member", None),
        P("blk", "member", None),
        P("blk", "member", None),
    )
    return jax.shard_map(
        body,
        mesh=mesh,
        in_specs=placed,
        out_specs=(P("member", "blk", None), P("member", "blk", None)),
        check_vma=False,
    )
```

```python
import jax
import jax.numpy as jnp
import numpy as np
from jax import lax
from jax.experimental import pallas as pl
from jax.experimental.pallas import tpu as pltpu
from jax.sharding import PartitionSpec as P

MESH = pl.DeviceIdType.MESH
EXP_GRP = 4
CAP = 6
PAD = 8
SHARDS = 8
COLS = 32
BLKS = 16
BF = jnp.bfloat16
F32 = jnp.float32
NT = (((1,), (1,)), ((), ()))
VMEM_SPEC = pl.BlockSpec(memory_space=pltpu.VMEM)
CHUNKS = 4


def loop(start, stop, step):
    def run(k, carry):
        step(k)
        return carry

    lax.fori_loop(start, stop, run, 0)


def greet(axis, me, n, meanwhile):
    barrier = pltpu.get_barrier_semaphore()
    loop(
        1,
        n,
        lambda k: pl.semaphore_signal(
            barrier, inc=1, device_id={axis: lax.rem(me + k, n)}, device_id_type=MESH
        ),
    )
    meanwhile()
    pl.semaphore_wait(barrier, n - 1)


def send(src, dst, send_sem, recv_sem, axis, peer):
    return pltpu.make_async_remote_copy(
        src_ref=src,
        dst_ref=dst,
        send_sem=send_sem,
        recv_sem=recv_sem,
        device_id={axis: peer},
        device_id_type=MESH,
    )


def row_pairs():
    pairs = COLS // BLKS
    for i in range(2 * BLKS):
        yield i // 2, i % 2, slice(pairs * i, pairs * (i + 1))


def flip(m, w):
    return m + w - 2 * w * lax.rem(m // w, 2)


def greet_few(axis, peers, meanwhile=lambda: None):
    barrier = pltpu.get_barrier_semaphore()
    for peer in peers:
        pl.semaphore_signal(barrier, inc=1, device_id={axis: peer}, device_id_type=MESH)
    meanwhile()
    pl.semaphore_wait(barrier, len(peers))


FAR_FIRST = (4, 3, 5, 2, 6, 1, 7)
NEAR_FIRST = (1, 7, 2, 6, 3, 5, 4)


def gather_kernel(x, g, out, send_sem, recv_sem, pass_send, pass_recv):
    me = lax.axis_index("blk")
    partner = flip(me, 1)
    ahead = {k: lax.rem(me + 2 * k, BLKS) for k in range(1, 8)}
    greet_few("blk", [ahead[k] for k in FAR_FIRST] + [partner])

    def first(k, peer):
        return [
            send(src.at[0], out.at[me, h], send_sem.at[h, k], recv_sem.at[h, k], "blk", peer)
            for h, src in enumerate((x, g))
        ]

    def passed(k, source):
        return send(
            out.at[source], out.at[source], pass_send.at[k], pass_recv.at[k], "blk", partner
        )

    direct = {k: first(k, ahead[k]) for k in FAR_FIRST}
    direct[0] = first(0, partner)
    for k in FAR_FIRST + (0,):
        for c in direct[k]:
            c.start()
    out[me, 0] = x[0]
    out[me, 1] = g[0]
    relays = []
    for k in NEAR_FIRST:
        for c in direct[k]:
            c.wait_recv()
        relay = passed(k, lax.rem(me + BLKS - 2 * k, BLKS))
        relay.start()
        relays.append(relay)
    for c in direct[0]:
        c.wait_recv()
    for k in FAR_FIRST + (0,):
        for c in direct[k]:
            c.wait_send()
    for relay in relays:
        relay.wait()


def swap_kernel(
    sums, combine, out_a, out_b, mixed, src, near, mid, far, send_sem, recv_sem, far_send, far_recv
):
    me = lax.axis_index("blk")
    partner = flip(me, 1)
    ahead = {k: lax.rem(me + 2 * k, BLKS) for k in range(8)}
    width = sums.shape[1] // SHARDS

    def mix(j):
        cols = pl.ds(pl.multiple_of(width * j, width), width)
        mixed[:, cols] = jnp.dot(
            combine[...],
            sums[:, cols].astype(F32),
            precision=lax.Precision.HIGHEST,
            preferred_element_type=F32,
        )

    def prepare():
        loop(0, SHARDS, mix)
        for p, h, at in row_pairs():
            src[p, h] = mixed[at].astype(BF)

    greet_few("blk", [ahead[k] for k in FAR_FIRST] + [partner], prepare)

    def pair(k):
        return send(
            src.at[flip(ahead[k], 1)],
            near.at[flip(ahead[k], 1) // 2],
            send_sem.at[k],
            recv_sem.at[k],
            "blk",
            partner,
        )

    def along(k):
        return send(mid.at[k], far.at[k], far_send.at[k], far_recv.at[k], "blk", ahead[k])

    order = FAR_FIRST + (0,)
    for k in order:
        pair(k).start()
    for k in order:
        pair(k).wait_recv()
        total = src[ahead[k]].astype(F32) + near[ahead[k] // 2].astype(F32)
        if k:
            mid[k] = total.astype(BF)
            along(k).start()
    for k in NEAR_FIRST:
        along(k).wait_recv()
        total = total + far[k].astype(F32)
    out_a[0] = total[0].astype(BF)
    out_b[0] = total[1].astype(BF)
    for k in order:
        pair(k).wait_send()
        if k:
            along(k).wait_send()


def layer_kernel(
    both_ref, picker, gate, up, down, pack, unpack, spread, out,
    picks, flat, src, rows_ref, w, acc, acc_rest, og, t1, s1, t2, s2, t3, home,
    send_sem, recv_sem, own_sem, w_sem, hop_send, hop_recv,
    c_send, c_recv, y_send, y_recv, x_send, x_recv, h_send, h_recv,
):
    me = lax.axis_index("member")
    width = flat.shape[1] // SHARDS
    lane = width // 4
    thin = width - lane
    n = w.shape[0] // 3
    rows = 2 * PAD
    dense = 2 * CAP
    per = COLS // CHUNKS
    mine = lax.rem(me, SHARDS)
    bit_c, bit_x, bit_y = lax.rem(me, 2), lax.rem(me // 2, 2), lax.rem(me // 4, 2)
    across, along, other = flip(me, 2), flip(me, 4), flip(me, 1)
    part_x, part_y = flip(mine, 2), flip(mine, 4)
    part_xy = flip(part_x, 4)

    loads = [
        pltpu.make_async_copy(ref.at[0], w.at[pl.ds(n * i, n)], w_sem.at[i])
        for i, ref in enumerate((gate, up, down))
    ]
    for load in loads:
        load.start()
    def some(size, at):
        return pl.ds(pl.multiple_of(size * at, size), size)

    def lanes(part):
        return some(width, part)

    def pick(j):
        sums = jnp.dot(picks[...], flat[:, lanes(j)].astype(BF), preferred_element_type=F32)
        tall = src.shape[0]
        for t in range(3):
            tile = sums[:tall, lane * t : lane * (t + 1)]
            tile = tile + sums[tall * (t + 1) : tall * (t + 2), thin:]
            src[:, some(lane, 3 * j + t)] = tile.astype(BF)

    def regroup():
        for p, h, at in row_pairs():
            flat[at] = both_ref[p, h].astype(F32)
        picks[...] = jnp.dot(spread[...], picker[...], preferred_element_type=F32).astype(BF)
        loop(0, SHARDS, pick)

    greet("member", me, COLS, regroup)

    def piece(peer):
        return src.at[some(rows, peer // SHARDS), some(thin, lax.rem(peer, SHARDS))]

    def place(col, part):
        return rows_ref.at[some(rows, col), some(thin, part)]

    slot = me // SHARDS

    def chunk(q):
        return lax.rem(slot + q + (q // 2) * (1 - 2 * (q % 2)), CHUNKS)

    def column(q, j):
        return per * chunk(q) + j

    def put(k):
        peer = column(k // per, lax.rem(mine + k, per))
        return send(
            piece(peer),
            place(me, lax.rem(peer, SHARDS)),
            send_sem.at[k],
            recv_sem.at[me],
            "member",
            peer,
        )

    def others(step):
        def run(c):
            @pl.when(c != me)
            def _():
                step(c)

        return run

    def arrived(c):
        send(
            place(c, mine), place(c, mine), send_sem.at[0], recv_sem.at[c], "member", other
        ).wait_recv()

    def hop(kind, q, origin, peer):
        part = rows_ref.at[some(rows * per, chunk(q)), some(thin, origin)]
        return send(part, part, hop_send.at[kind, q], hop_recv.at[kind, q], "member", peer)

    to_x = lambda q: hop(0, q, mine, across)
    to_y = lambda q: hop(1, q, mine, along)

    def route(q, relay_y, relay_x):
        late = (q + CHUNKS - 1) // CHUNKS
        return (1 - late) * relay_y + late * relay_x

    relay = lambda q: hop(2, q, route(q, part_x, part_y), route(q, along, across))
    origins = (mine, part_x, part_y, part_xy)
    core = lambda i, q: hop(3 + i, q, origins[i], other)

    def multiply(q, origin, fresh=False):
        span = some(rows * per, q)
        left = rows_ref[some(rows * per, chunk(q)), some(thin, origin)]
        near = w[:, pl.ds(pl.multiple_of(width * origin, width), thin)]
        rest = w[:, pl.ds(pl.multiple_of(width * origin + thin, lane), lane)]
        term = lax.dot_general(left, near, NT, preferred_element_type=F32)
        acc[span] = term if fresh else acc[span] + term
        tiles = jnp.concatenate([left[:, lane * t : lane * (t + 1)] for t in range(3)], axis=0)
        term = lax.dot_general(tiles, rest, NT, preferred_element_type=F32)
        for t in range(3):
            part = term[rows * per * t : rows * per * (t + 1)]
            acc_rest[t, span] = part if fresh else acc_rest[t, span] + part

    own = pltpu.make_async_copy(piece(me), place(me, mine), own_sem.at[0])
    loop(1, COLS, lambda k: put(k).start())
    own.start()
    own.wait()

    def phase_own(q):
        loop(0, per, lambda j: others(arrived)(column(q, j)))
        to_x(q).start()
        to_y(q).start()
        core(0, q).start()

    def phase_near(q):
        to_x(q).wait_recv()
        core(1, q).start()
        to_y(q).wait_recv()
        relay(q).start()
        core(2, q).start()

    def first_blocks(q):
        multiply(q, mine, True)
        multiply(q, part_x)
        multiply(q, part_y)

    def phase_core(q):
        for i in range(3):
            core(i, q).wait_recv()
            multiply(q, flip(origins[i], 1))

    def swap_core(q, h):
        return send(
            og.at[some(dense * per, q), lanes(2 * h + 1 - bit_c)],
            t1.at[h, some(dense * per, q)],
            c_send.at[q, h],
            c_recv.at[q, h],
            "member",
            other,
        )

    def near_done(q):
        relay(q).wait_recv()
        core(3, q).start()
        multiply(q, part_xy)

    def finish(q):
        core(3, q).wait_recv()
        multiply(q, flip(part_xy, 1))
        at = lax.broadcasted_iota(jnp.int32, (per, PAD, n), 1)

        def whole(i, h):
            cols = slice(n * i, n * (i + 1))
            value = acc[some(rows * per, q), cols].reshape(per, 2, PAD, n)[:, h]
            for t in range(3):
                rest = acc_rest[t, some(rows * per, q), cols].reshape(per, 2, PAD, n)[:, h]
                here = (at >= 2 * t) & (at < 2 * t + 2)
                value = value + jnp.where(here, pltpu.roll(rest, 2 * t + 2, 1), 0.0)
            return value.reshape(per * PAD, n)

        pre_gate, pre_up, d_hidden = whole(0, 0), whole(1, 0), whole(2, 1)
        logistic = jax.nn.sigmoid(pre_gate)
        activated = pre_gate * logistic
        hidden = (activated * pre_up).astype(BF)
        grad_gate = (
            d_hidden * pre_up * logistic * (1.0 + pre_gate * (1.0 - logistic))
        ).astype(BF)
        grad_up = (d_hidden * activated).astype(BF)
        left = [
            jnp.dot(pack[h], v, preferred_element_type=F32).astype(BF)
            for h, v in ((1, grad_gate), (1, grad_up), (0, hidden))
        ]
        left = jnp.concatenate(left, axis=1)

        def second(k):
            cols = lanes(k)
            total = jnp.dot(left, w[:, cols], preferred_element_type=F32)
            og[some(dense * per, q), cols] = total.astype(BF)

        loop(0, SHARDS, second)
        for h in range(4):
            swap_core(q, h).start()

    loop(0, CHUNKS, phase_own)
    loop(0, CHUNKS, phase_near)
    for load in loads:
        load.wait()
    loop(0, CHUNKS, first_blocks)
    loop(0, CHUNKS, phase_core)
    near_done(0)
    near_done(1)
    finish(0)

    def span(q):
        return some(dense * per, q)

    def swap_pair(q, i):
        return send(
            s1.at[route(q, 2 * (1 - bit_y) + i, 2 * i + 1 - bit_x), span(q)],
            t2.at[i, span(q)],
            y_send.at[q, i],
            y_recv.at[q, i],
            "member",
            route(q, along, across),
        )

    def swap_last(q):
        return send(
            s2.at[1 - route(q, bit_x, bit_y), span(q)],
            t3.at[span(q)],
            x_send.at[q],
            x_recv.at[q],
            "member",
            route(q, across, along),
        )

    def spot(source):
        return out.at[some(rows, source // SHARDS), lanes(lax.rem(source, SHARDS))]

    def deliver(q, j):
        c = column(q, j)
        return send(
            home.at[some(rows, per * q + j)], spot(me), h_send.at[c], h_recv.at[me], "member", c
        )

    def deliver_all(q, step):
        loop(0, per, lambda j: others(lambda c: step(deliver(q, j)))(column(q, j)))

    def add_core(q):
        for h in range(4):
            swap_core(q, h).wait_recv()
            total = og[span(q), lanes(2 * h + bit_c)].astype(F32) + t1[h, span(q)].astype(F32)
            s1[h, span(q)] = total.astype(BF)
        for i in range(2):
            swap_pair(q, i).start()

    def add_pair(q):
        for i in range(2):
            swap_pair(q, i).wait_recv()
            kept = s1[route(q, 2 * bit_y + i, 2 * i + bit_x), span(q)]
            s2[i, span(q)] = (kept.astype(F32) + t2[i, span(q)].astype(F32)).astype(BF)
        swap_last(q).start()

    def add_last(q):
        swap_last(q).wait_recv()
        total = s2[route(q, bit_x, bit_y), span(q)].astype(F32) + t3[span(q)].astype(F32)
        wide = jnp.dot(unpack[...], total.astype(BF), preferred_element_type=F32)
        home[some(rows * per, q)] = wide.astype(BF)
        deliver_all(q, lambda copy: copy.start())

    def step(q):
        near_done(q)
        finish(q - 1)
        add_core(q - 2)

    loop(2, CHUNKS, step)
    finish(CHUNKS - 1)
    add_core(CHUNKS - 2)
    add_core(CHUNKS - 1)
    loop(0, CHUNKS, add_pair)
    loop(1, CHUNKS, add_last)
    add_last(0)
    last = pltpu.make_async_copy(home.at[some(rows, mine)], spot(me), own_sem.at[1])
    last.start()

    def drain(q):
        to_x(q).wait_send()
        to_y(q).wait_send()
        relay(q).wait_send()
        for i in range(4):
            core(i, q).wait_send()
            swap_core(q, i).wait_send()
        for i in range(2):
            swap_pair(q, i).wait_send()
        swap_last(q).wait_send()

    def landed(c):
        send(
            home.at[some(rows, 0)], spot(c), h_send.at[0], h_recv.at[c], "member", other
        ).wait_recv()

    loop(1, COLS, lambda k: put(k).wait_send())
    loop(0, CHUNKS, drain)
    loop(0, CHUNKS, lambda q: deliver_all(q, lambda copy: copy.wait_send()))
    loop(0, COLS, others(landed))
    last.wait()


def remote_call(kernel, specs, shape, scratch, ident):
    return pl.pallas_call(
        kernel,
        out_shape=jax.tree.map(lambda dims: jax.ShapeDtypeStruct(dims, BF), shape,
                               is_leaf=lambda v: isinstance(v[0], int)),
        in_specs=specs,
        out_specs=jax.tree.map(lambda dims: VMEM_SPEC, shape,
                               is_leaf=lambda v: isinstance(v[0], int)),
        scratch_shapes=scratch,
        compiler_params=pltpu.CompilerParams(collective_id=ident, has_side_effects=True),
    )


def packing():
    per = COLS // CHUNKS
    pack = np.zeros((2, per * 2 * CAP, per * PAD), np.float32)
    unpack = np.zeros((per * 2 * PAD, per * 2 * CAP), np.float32)
    for c in range(per):
        for h in range(2):
            for r in range(CAP):
                pack[h, (c * 2 + h) * CAP + r, c * PAD + r] = 1
                unpack[(c * 2 + h) * PAD + r, (c * 2 + h) * CAP + r] = 1
    spread = np.zeros((4, EXP_GRP * 2, PAD, EXP_GRP * 2, PAD), np.float32)
    for e in range(EXP_GRP * 2):
        for r in range(CAP):
            spread[0, e, r, e, r] = 1
            spread[1 + r // 2, e, CAP + r % 2, e, r] = 1
    spread = spread.reshape(4 * EXP_GRP * 2 * PAD, EXP_GRP * 2 * PAD)
    return jnp.asarray(pack, BF), jnp.asarray(unpack, BF), jnp.asarray(spread, BF)


def body(tokens, cotangent, routes, gate_wts, w_gate, w_up, w_down):
    width = tokens.shape[2]
    dma = pltpu.SemaphoreType.DMA
    pack, unpack, spread = packing()

    experts = lax.axis_index("blk") * EXP_GRP + jnp.arange(EXP_GRP, dtype=jnp.int32)
    match = routes[0][None] == experts[:, None, None]
    named = jnp.sum(match.astype(F32), axis=2)
    weight = jnp.sum(jnp.where(match, gate_wts[0][None], 0.0), axis=2)
    square = (EXP_GRP, COLS, COLS)
    earlier = lax.broadcasted_iota(jnp.int32, square, 2) < lax.broadcasted_iota(jnp.int32, square, 1)
    rank = jnp.sum(jnp.where(earlier, named[:, None, :], 0.0), axis=2)
    places = jnp.arange(PAD, dtype=jnp.int32).astype(F32)
    taken = jnp.where(
        (rank[:, None, :] == places[None, :, None]) & (named[:, None, :] > 0), 1.0, 0.0
    )
    both = np.eye(2, dtype=np.float32)[None, :, None, None, :, None]

    def table(values):
        grid = values.reshape(EXP_GRP, 1, PAD, BLKS, 1, COLS // BLKS) * both
        return grid.reshape(EXP_GRP * 2 * PAD, 2 * COLS)

    picker = table(taken).astype(BF)
    combine = table(taken * weight[:, None, :]).T

    pairs = COLS // BLKS
    column = remote_call(
        gather_kernel,
        [VMEM_SPEC] * 2,
        (BLKS, 2, pairs, width),
        [dma((2, 8)), dma((2, 8)), dma((8,)), dma((8,))],
        0,
    )(tokens, cotangent)
    dense, padded, piece = COLS * 2 * CAP, COLS * 2 * PAD, width // SHARDS
    hidden = w_gate.shape[1]
    sums = remote_call(
        layer_kernel,
        [VMEM_SPEC] * 2 + [pl.BlockSpec(memory_space=pl.ANY)] * 3 + [VMEM_SPEC] * 3,
        (EXP_GRP * 2 * PAD, width),
        [
            pltpu.VMEM((8 * EXP_GRP * PAD, 2 * COLS), BF),
            pltpu.VMEM((2 * COLS, width), F32),
            pltpu.VMEM((EXP_GRP * 2 * PAD, width // 4 * 3), BF),
            pltpu.VMEM((padded, width // 4 * 3), BF),
            pltpu.VMEM((3 * hidden, width), BF),
            pltpu.VMEM((padded, 3 * hidden), F32),
            pltpu.VMEM((3, padded, 3 * hidden), F32),
            pltpu.VMEM((dense, width), BF),
            pltpu.VMEM((4, dense, piece), BF),
            pltpu.VMEM((4, dense, piece), BF),
            pltpu.VMEM((2, dense, piece), BF),
            pltpu.VMEM((2, dense, piece), BF),
            pltpu.VMEM((dense, piece), BF),
            pltpu.VMEM((padded, piece), BF),
            dma((COLS,)),
            dma((COLS,)),
            dma((2,)),
            dma((3,)),
            dma((7, CHUNKS)),
            dma((7, CHUNKS)),
            dma((CHUNKS, 4)),
            dma((CHUNKS, 4)),
            dma((CHUNKS, 2)),
            dma((CHUNKS, 2)),
            dma((CHUNKS,)),
            dma((CHUNKS,)),
            dma((COLS,)),
            dma((COLS,)),
        ],
        1,
    )(column, picker, w_gate, w_up, w_down, pack, unpack, spread)
    half = (BLKS // 2, 2, pairs, width)
    return remote_call(
        swap_kernel,
        [VMEM_SPEC] * 2,
        ((1, pairs, width), (1, pairs, width)),
        [pltpu.VMEM((2 * COLS, width), F32), pltpu.VMEM((BLKS, 2, pairs, width), BF)]
        + [pltpu.VMEM(half, BF)] * 3
        + [dma((8,))] * 4,
        2,
    )(sums, combine)


def solution(mesh):
    placed = (
        P("member", "blk", None),
        P("member", "blk", None),
        P("member", None, None),
        P("member", None, None),
        P("blk", "member", None),
        P("blk", "member", None),
        P("blk", "member", None),
    )
    return jax.shard_map(
        body,
        mesh=mesh,
        in_specs=placed,
        out_specs=(P("member", "blk", None), P("member", "blk", None)),
        check_vma=False,
    )
```

```python
import jax
import jax.numpy as jnp
import numpy as np
from jax import lax
from jax.experimental import pallas as pl
from jax.experimental.pallas import tpu as pltpu
from jax.sharding import PartitionSpec as P

MESH = pl.DeviceIdType.MESH
EXP_GRP = 4
CAP = 6
PAD = 8
SHARDS = 8
COLS = 32
BLKS = 16
BF = jnp.bfloat16
F32 = jnp.float32
NT = (((1,), (1,)), ((), ()))
VMEM_SPEC = pl.BlockSpec(memory_space=pltpu.VMEM)
CHUNKS = 4


def loop(start, stop, step):
    def run(k, carry):
        step(k)
        return carry

    lax.fori_loop(start, stop, run, 0)


def greet(axis, me, n, meanwhile):
    barrier = pltpu.get_barrier_semaphore()
    loop(
        1,
        n,
        lambda k: pl.semaphore_signal(
            barrier, inc=1, device_id={axis: lax.rem(me + k, n)}, device_id_type=MESH
        ),
    )
    meanwhile()
    pl.semaphore_wait(barrier, n - 1)


def send(src, dst, send_sem, recv_sem, axis, peer):
    return pltpu.make_async_remote_copy(
        src_ref=src,
        dst_ref=dst,
        send_sem=send_sem,
        recv_sem=recv_sem,
        device_id={axis: peer},
        device_id_type=MESH,
    )


def row_pairs():
    pairs = COLS // BLKS
    for i in range(2 * BLKS):
        yield i // 2, i % 2, slice(pairs * i, pairs * (i + 1))


def flip(m, w):
    return m + w - 2 * w * lax.rem(m // w, 2)


def greet_few(axis, peers, meanwhile=lambda: None):
    barrier = pltpu.get_barrier_semaphore()
    for peer in peers:
        pl.semaphore_signal(barrier, inc=1, device_id={axis: peer}, device_id_type=MESH)
    meanwhile()
    pl.semaphore_wait(barrier, len(peers))


FAR_FIRST = (4, 3, 5, 2, 6, 1, 7)
NEAR_FIRST = (1, 7, 2, 6, 3, 5, 4)


def gather_kernel(x, g, out, send_sem, recv_sem, pass_send, pass_recv):
    me = lax.axis_index("blk")
    partner = flip(me, 1)
    ahead = {k: lax.rem(me + 2 * k, BLKS) for k in range(1, 8)}
    greet_few("blk", [ahead[k] for k in FAR_FIRST] + [partner])

    def first(k, peer):
        return [
            send(src.at[0], out.at[me, h], send_sem.at[h, k], recv_sem.at[h, k], "blk", peer)
            for h, src in enumerate((x, g))
        ]

    def passed(k, source):
        return send(
            out.at[source], out.at[source], pass_send.at[k], pass_recv.at[k], "blk", partner
        )

    direct = {k: first(k, ahead[k]) for k in FAR_FIRST}
    direct[0] = first(0, partner)
    for k in FAR_FIRST + (0,):
        for c in direct[k]:
            c.start()
    out[me, 0] = x[0]
    out[me, 1] = g[0]
    relays = []
    for k in NEAR_FIRST:
        for c in direct[k]:
            c.wait_recv()
        relay = passed(k, lax.rem(me + BLKS - 2 * k, BLKS))
        relay.start()
        relays.append(relay)
    for c in direct[0]:
        c.wait_recv()
    for k in FAR_FIRST + (0,):
        for c in direct[k]:
            c.wait_send()
    for relay in relays:
        relay.wait()


def swap_kernel(
    sums, combine, out_a, out_b, mixed, src, near, mid, far, send_sem, recv_sem, far_send, far_recv
):
    me = lax.axis_index("blk")
    partner = flip(me, 1)
    ahead = {k: lax.rem(me + 2 * k, BLKS) for k in range(8)}
    width = sums.shape[1] // SHARDS

    def mix(j):
        cols = pl.ds(pl.multiple_of(width * j, width), width)
        mixed[:, cols] = jnp.dot(
            combine[...],
            sums[:, cols].astype(F32),
            precision=lax.Precision.HIGHEST,
            preferred_element_type=F32,
        )

    def prepare():
        loop(0, SHARDS, mix)
        for p, h, at in row_pairs():
            src[p, h] = mixed[at].astype(BF)

    greet_few("blk", [ahead[k] for k in FAR_FIRST] + [partner], prepare)

    def pair(k):
        return send(
            src.at[flip(ahead[k], 1)],
            near.at[flip(ahead[k], 1) // 2],
            send_sem.at[k],
            recv_sem.at[k],
            "blk",
            partner,
        )

    def along(k):
        return send(mid.at[k], far.at[k], far_send.at[k], far_recv.at[k], "blk", ahead[k])

    order = FAR_FIRST + (0,)
    for k in order:
        pair(k).start()
    for k in order:
        pair(k).wait_recv()
        total = src[ahead[k]].astype(F32) + near[ahead[k] // 2].astype(F32)
        if k:
            mid[k] = total.astype(BF)
            along(k).start()
    for k in NEAR_FIRST:
        along(k).wait_recv()
        total = total + far[k].astype(F32)
    out_a[0] = total[0].astype(BF)
    out_b[0] = total[1].astype(BF)
    for k in order:
        pair(k).wait_send()
        if k:
            along(k).wait_send()


def layer_kernel(
    both_ref, picker, gate, up, down, pack, unpack, spread, out,
    picks, flat, src, rows_ref, w, acc, acc_rest, og, t1, s1, t2, s2, t3, home,
    send_sem, recv_sem, own_sem, w_sem, hop_send, hop_recv,
    c_send, c_recv, y_send, y_recv, x_send, x_recv, h_send, h_recv,
):
    me = lax.axis_index("member")
    width = flat.shape[1] // SHARDS
    lane = width // 4
    thin = width - lane
    n = w.shape[0] // 3
    rows = 2 * PAD
    dense = 2 * CAP
    per = COLS // CHUNKS
    mine = lax.rem(me, SHARDS)
    bit_c, bit_x, bit_y = lax.rem(me, 2), lax.rem(me // 2, 2), lax.rem(me // 4, 2)
    across, along, other = flip(me, 2), flip(me, 4), flip(me, 1)
    part_x, part_y = flip(mine, 2), flip(mine, 4)
    part_xy = flip(part_x, 4)

    loads = [
        pltpu.make_async_copy(ref.at[0], w.at[pl.ds(n * i, n)], w_sem.at[i])
        for i, ref in enumerate((gate, up, down))
    ]
    for load in loads:
        load.start()
    def some(size, at):
        return pl.ds(pl.multiple_of(size * at, size), size)

    def lanes(part):
        return some(width, part)

    def pick(j):
        sums = jnp.dot(picks[...], flat[:, lanes(j)].astype(BF), preferred_element_type=F32)
        tall = src.shape[0]
        for t in range(3):
            tile = sums[:tall, lane * t : lane * (t + 1)]
            tile = tile + sums[tall * (t + 1) : tall * (t + 2), thin:]
            src[:, some(lane, 3 * j + t)] = tile.astype(BF)

    def regroup():
        for p, h, at in row_pairs():
            flat[at] = both_ref[p, h].astype(F32)
        picks[...] = jnp.dot(spread[...], picker[...], preferred_element_type=F32).astype(BF)
        loop(0, SHARDS, pick)

    greet("member", me, COLS, regroup)

    def piece(peer):
        return src.at[some(rows, peer // SHARDS), some(thin, lax.rem(peer, SHARDS))]

    def place(col, part):
        return rows_ref.at[some(rows, col), some(thin, part)]

    slot = me // SHARDS

    def chunk(q):
        return lax.rem(slot + q + (q // 2) * (1 - 2 * (q % 2)), CHUNKS)

    def column(q, j):
        return per * chunk(q) + j

    def put(k):
        peer = column(k // per, lax.rem(mine + k, per))
        return send(
            piece(peer),
            place(me, lax.rem(peer, SHARDS)),
            send_sem.at[k],
            recv_sem.at[me],
            "member",
            peer,
        )

    def others(step):
        def run(c):
            @pl.when(c != me)
            def _():
                step(c)

        return run

    def arrived(c):
        send(
            place(c, mine), place(c, mine), send_sem.at[0], recv_sem.at[c], "member", other
        ).wait_recv()

    def hop(kind, q, origin, peer):
        part = rows_ref.at[some(rows * per, chunk(q)), some(thin, origin)]
        return send(part, part, hop_send.at[kind, q], hop_recv.at[kind, q], "member", peer)

    to_x = lambda q: hop(0, q, mine, across)
    to_y = lambda q: hop(1, q, mine, along)

    def route(q, relay_y, relay_x):
        late = (q + CHUNKS - 1) // CHUNKS
        return (1 - late) * relay_y + late * relay_x

    relay = lambda q: hop(2, q, route(q, part_x, part_y), route(q, along, across))
    origins = (mine, part_x, part_y, part_xy)
    core = lambda i, q: hop(3 + i, q, origins[i], other)

    def multiply(q, origin, fresh=False):
        span = some(rows * per, q)
        left = rows_ref[some(rows * per, chunk(q)), some(thin, origin)]
        near = w[:, pl.ds(pl.multiple_of(width * origin, width), thin)]
        rest = w[:, pl.ds(pl.multiple_of(width * origin + thin, lane), lane)]
        term = lax.dot_general(left, near, NT, preferred_element_type=F32)
        acc[span] = term if fresh else acc[span] + term
        tiles = jnp.concatenate([left[:, lane * t : lane * (t + 1)] for t in range(3)], axis=0)
        term = lax.dot_general(tiles, rest, NT, preferred_element_type=F32)
        for t in range(3):
            part = term[rows * per * t : rows * per * (t + 1)]
            acc_rest[t, span] = part if fresh else acc_rest[t, span] + part

    own = pltpu.make_async_copy(piece(me), place(me, mine), own_sem.at[0])
    loop(1, COLS, lambda k: put(k).start())
    own.start()
    own.wait()

    def phase_own(q):
        loop(0, per, lambda j: others(arrived)(column(q, j)))
        to_x(q).start()
        to_y(q).start()
        core(0, q).start()
        multiply(q, mine, True)

    def phase_near(q):
        to_x(q).wait_recv()
        core(1, q).start()
        to_y(q).wait_recv()
        relay(q).start()
        core(2, q).start()
        multiply(q, part_x)
        multiply(q, part_y)

    def phase_core(q):
        for i in range(3):
            core(i, q).wait_recv()
            multiply(q, flip(origins[i], 1))

    def swap_core(q, h):
        return send(
            og.at[some(dense * per, q), lanes(2 * h + 1 - bit_c)],
            t1.at[h, some(dense * per, q)],
            c_send.at[q, h],
            c_recv.at[q, h],
            "member",
            other,
        )

    def near_done(q):
        relay(q).wait_recv()
        core(3, q).start()
        multiply(q, part_xy)

    def finish(q):
        core(3, q).wait_recv()
        multiply(q, flip(part_xy, 1))
        at = lax.broadcasted_iota(jnp.int32, (per, PAD, n), 1)

        def whole(i, h):
            cols = slice(n * i, n * (i + 1))
            value = acc[some(rows * per, q), cols].reshape(per, 2, PAD, n)[:, h]
            for t in range(3):
                rest = acc_rest[t, some(rows * per, q), cols].reshape(per, 2, PAD, n)[:, h]
                here = (at >= 2 * t) & (at < 2 * t + 2)
                value = value + jnp.where(here, pltpu.roll(rest, 2 * t + 2, 1), 0.0)
            return value.reshape(per * PAD, n)

        pre_gate, pre_up, d_hidden = whole(0, 0), whole(1, 0), whole(2, 1)
        logistic = jax.nn.sigmoid(pre_gate)
        activated = pre_gate * logistic
        hidden = (activated * pre_up).astype(BF)
        grad_gate = (
            d_hidden * pre_up * logistic * (1.0 + pre_gate * (1.0 - logistic))
        ).astype(BF)
        grad_up = (d_hidden * activated).astype(BF)
        left = [
            jnp.dot(pack[h], v, preferred_element_type=F32).astype(BF)
            for h, v in ((1, grad_gate), (1, grad_up), (0, hidden))
        ]
        left = jnp.concatenate(left, axis=1)

        def second(k):
            cols = lanes(k)
            total = jnp.dot(left, w[:, cols], preferred_element_type=F32)
            og[some(dense * per, q), cols] = total.astype(BF)

        loop(0, SHARDS, second)
        for h in range(4):
            swap_core(q, h).start()

    for load in loads:
        load.wait()
    loop(0, CHUNKS, phase_own)
    loop(0, CHUNKS, phase_near)
    loop(0, CHUNKS, phase_core)
    near_done(0)
    near_done(1)
    finish(0)

    def span(q):
        return some(dense * per, q)

    def swap_pair(q, i):
        return send(
            s1.at[route(q, 2 * (1 - bit_y) + i, 2 * i + 1 - bit_x), span(q)],
            t2.at[i, span(q)],
            y_send.at[q, i],
            y_recv.at[q, i],
            "member",
            route(q, along, across),
        )

    def swap_last(q):
        return send(
            s2.at[1 - route(q, bit_x, bit_y), span(q)],
            t3.at[span(q)],
            x_send.at[q],
            x_recv.at[q],
            "member",
            route(q, across, along),
        )

    def spot(source):
        return out.at[some(rows, source // SHARDS), lanes(lax.rem(source, SHARDS))]

    def deliver(q, j):
        c = column(q, j)
        return send(
            home.at[some(rows, per * q + j)], spot(me), h_send.at[c], h_recv.at[me], "member", c
        )

    def deliver_all(q, step):
        loop(0, per, lambda j: others(lambda c: step(deliver(q, j)))(column(q, j)))

    def add_core(q):
        for h in range(4):
            swap_core(q, h).wait_recv()
            total = og[span(q), lanes(2 * h + bit_c)].astype(F32) + t1[h, span(q)].astype(F32)
            s1[h, span(q)] = total.astype(BF)
        for i in range(2):
            swap_pair(q, i).start()

    def add_pair(q):
        for i in range(2):
            swap_pair(q, i).wait_recv()
            kept = s1[route(q, 2 * bit_y + i, 2 * i + bit_x), span(q)]
            s2[i, span(q)] = (kept.astype(F32) + t2[i, span(q)].astype(F32)).astype(BF)
        swap_last(q).start()

    def add_last(q):
        swap_last(q).wait_recv()
        total = s2[route(q, bit_x, bit_y), span(q)].astype(F32) + t3[span(q)].astype(F32)
        wide = jnp.dot(unpack[...], total.astype(BF), preferred_element_type=F32)
        home[some(rows * per, q)] = wide.astype(BF)
        deliver_all(q, lambda copy: copy.start())

    def step(q):
        near_done(q)
        finish(q - 1)
        add_core(q - 2)

    loop(2, CHUNKS, step)
    finish(CHUNKS - 1)
    add_core(CHUNKS - 2)
    add_core(CHUNKS - 1)
    loop(0, CHUNKS, add_pair)
    loop(1, CHUNKS, add_last)
    add_last(0)
    last = pltpu.make_async_copy(home.at[some(rows, mine)], spot(me), own_sem.at[1])
    last.start()

    def drain(q):
        to_x(q).wait_send()
        to_y(q).wait_send()
        relay(q).wait_send()
        for i in range(4):
            core(i, q).wait_send()
            swap_core(q, i).wait_send()
        for i in range(2):
            swap_pair(q, i).wait_send()
        swap_last(q).wait_send()

    def landed(c):
        send(
            home.at[some(rows, 0)], spot(c), h_send.at[0], h_recv.at[c], "member", other
        ).wait_recv()

    loop(1, COLS, lambda k: put(k).wait_send())
    loop(0, CHUNKS, drain)
    loop(0, CHUNKS, lambda q: deliver_all(q, lambda copy: copy.wait_send()))
    loop(0, COLS, others(landed))
    last.wait()


def remote_call(kernel, specs, shape, scratch, ident):
    return pl.pallas_call(
        kernel,
        out_shape=jax.tree.map(lambda dims: jax.ShapeDtypeStruct(dims, BF), shape,
                               is_leaf=lambda v: isinstance(v[0], int)),
        in_specs=specs,
        out_specs=jax.tree.map(lambda dims: VMEM_SPEC, shape,
                               is_leaf=lambda v: isinstance(v[0], int)),
        scratch_shapes=scratch,
        compiler_params=pltpu.CompilerParams(collective_id=ident, has_side_effects=True),
    )


def packing():
    per = COLS // CHUNKS
    pack = np.zeros((2, per * 2 * CAP, per * PAD), np.float32)
    unpack = np.zeros((per * 2 * PAD, per * 2 * CAP), np.float32)
    for c in range(per):
        for h in range(2):
            for r in range(CAP):
                pack[h, (c * 2 + h) * CAP + r, c * PAD + r] = 1
                unpack[(c * 2 + h) * PAD + r, (c * 2 + h) * CAP + r] = 1
    spread = np.zeros((4, EXP_GRP * 2, PAD, EXP_GRP * 2, PAD), np.float32)
    for e in range(EXP_GRP * 2):
        for r in range(CAP):
            spread[0, e, r, e, r] = 1
            spread[1 + r // 2, e, CAP + r % 2, e, r] = 1
    spread = spread.reshape(4 * EXP_GRP * 2 * PAD, EXP_GRP * 2 * PAD)
    return jnp.asarray(pack, BF), jnp.asarray(unpack, BF), jnp.asarray(spread, BF)


def body(tokens, cotangent, routes, gate_wts, w_gate, w_up, w_down):
    width = tokens.shape[2]
    dma = pltpu.SemaphoreType.DMA
    pack, unpack, spread = packing()

    experts = lax.axis_index("blk") * EXP_GRP + jnp.arange(EXP_GRP, dtype=jnp.int32)
    match = routes[0][None] == experts[:, None, None]
    named = jnp.sum(match.astype(F32), axis=2)
    weight = jnp.sum(jnp.where(match, gate_wts[0][None], 0.0), axis=2)
    square = (EXP_GRP, COLS, COLS)
    earlier = lax.broadcasted_iota(jnp.int32, square, 2) < lax.broadcasted_iota(jnp.int32, square, 1)
    rank = jnp.sum(jnp.where(earlier, named[:, None, :], 0.0), axis=2)
    places = jnp.arange(PAD, dtype=jnp.int32).astype(F32)
    taken = jnp.where(
        (rank[:, None, :] == places[None, :, None]) & (named[:, None, :] > 0), 1.0, 0.0
    )
    both = np.eye(2, dtype=np.float32)[None, :, None, None, :, None]

    def table(values):
        grid = values.reshape(EXP_GRP, 1, PAD, BLKS, 1, COLS // BLKS) * both
        return grid.reshape(EXP_GRP * 2 * PAD, 2 * COLS)

    picker = table(taken).astype(BF)
    combine = table(taken * weight[:, None, :]).T

    pairs = COLS // BLKS
    column = remote_call(
        gather_kernel,
        [VMEM_SPEC] * 2,
        (BLKS, 2, pairs, width),
        [dma((2, 8)), dma((2, 8)), dma((8,)), dma((8,))],
        0,
    )(tokens, cotangent)
    dense, padded, piece = COLS * 2 * CAP, COLS * 2 * PAD, width // SHARDS
    hidden = w_gate.shape[1]
    sums = remote_call(
        layer_kernel,
        [VMEM_SPEC] * 2 + [pl.BlockSpec(memory_space=pl.ANY)] * 3 + [VMEM_SPEC] * 3,
        (EXP_GRP * 2 * PAD, width),
        [
            pltpu.VMEM((8 * EXP_GRP * PAD, 2 * COLS), BF),
            pltpu.VMEM((2 * COLS, width), F32),
            pltpu.VMEM((EXP_GRP * 2 * PAD, width // 4 * 3), BF),
            pltpu.VMEM((padded, width // 4 * 3), BF),
            pltpu.VMEM((3 * hidden, width), BF),
            pltpu.VMEM((padded, 3 * hidden), F32),
            pltpu.VMEM((3, padded, 3 * hidden), F32),
            pltpu.VMEM((dense, width), BF),
            pltpu.VMEM((4, dense, piece), BF),
            pltpu.VMEM((4, dense, piece), BF),
            pltpu.VMEM((2, dense, piece), BF),
            pltpu.VMEM((2, dense, piece), BF),
            pltpu.VMEM((dense, piece), BF),
            pltpu.VMEM((padded, piece), BF),
            dma((COLS,)),
            dma((COLS,)),
            dma((2,)),
            dma((3,)),
            dma((7, CHUNKS)),
            dma((7, CHUNKS)),
            dma((CHUNKS, 4)),
            dma((CHUNKS, 4)),
            dma((CHUNKS, 2)),
            dma((CHUNKS, 2)),
            dma((CHUNKS,)),
            dma((CHUNKS,)),
            dma((COLS,)),
            dma((COLS,)),
        ],
        1,
    )(column, picker, w_gate, w_up, w_down, pack, unpack, spread)
    half = (BLKS // 2, 2, pairs, width)
    return remote_call(
        swap_kernel,
        [VMEM_SPEC] * 2,
        ((1, pairs, width), (1, pairs, width)),
        [pltpu.VMEM((2 * COLS, width), F32), pltpu.VMEM((BLKS, 2, pairs, width), BF)]
        + [pltpu.VMEM(half, BF)] * 3
        + [dma((8,))] * 4,
        2,
    )(sums, combine)


def solution(mesh):
    placed = (
        P("member", "blk", None),
        P("member", "blk", None),
        P("member", None, None),
        P("member", None, None),
        P("blk", "member", None),
        P("blk", "member", None),
        P("blk", "member", None),
    )
    return jax.shard_map(
        body,
        mesh=mesh,
        in_specs=placed,
        out_specs=(P("member", "blk", None), P("member", "blk", None)),
        check_vma=False,
    )
```
